256 devices in a mesh: grid: 16 (over z, core), pencil: 16 (over y, x).
Axes of the slice: x: 4, y: 4, z: 8, core: 2. Of those that a mesh axis runs over, the one named last changes fastest.
Arguments:
- field: bfloat16 [16, 512, 256, 128], P('grid', 'pencil'), may hold values from -6 to 6
- levels: int32 [16, 3], P('grid'), may hold values from 7 to 9, as said below
- coefficients: int32 [16], P('grid'), may hold values from -2 to 2
- failed: int32 [16], P('grid'), may hold values 0 or 1
- owner_map: int32 [64], replicated, may hold values from -1 to 47, as said below
- velocity: float32 [3], replicated, may hold values from -1 to 1
- diffusivity: float32 [3], replicated, may hold values from 0.5 to 4
Outputs:
- combined: float32 [48, 2, 128, 4096], P('grid', None, 'pencil')
The draws below stay inside these ranges and needn't reach their ends.
Inputs may be any that keep to these rules, and one draw needn't show every extreme that they name: `levels`: each row is (9, 8, 7) or (8, 9, 7); each occurs in 8 rows. `owner_map`: blocks held by no grid map to -1; every other block maps to a distinct row, and every row is named once. Owner o holds rows o * 3 to o * 3 + 2: 1 block held by grids of both level vectors and 1 held only by grids of each one, so every grid holds exactly 2 of each owner's blocks.
All inputs are finite; a program needn't handle non-finite values. No bound on the sum of `failed` on one device may be relied on, other than what follows from the above.
Results may differ from the reference program's by a relative error of at most 0.0056.
Values may be sent and summed in bfloat16 or wider, within the bound.
A program may use at most 128 MiB of HBM per device.

```python
import math
import jax
import jax.numpy as jnp
from jax import lax

LEV_MID = 8
LEV_Z = 7
SIDE_MID = 256
SIDE_HI = 512
SIDE_Z = 128
BLOCK = 64
GRIDS = 16
SLOTS = 3


def draw_levels(key, part):
    ordering = jax.random.permutation(key, GRIDS) % 2
    first_kind = jnp.array([LEV_MID + 1, LEV_MID, LEV_Z], jnp.int32)
    second_kind = jnp.array([LEV_MID, LEV_MID + 1, LEV_Z], jnp.int32)
    return jnp.where((ordering == 0)[:, None], first_kind[None, :], second_kind[None, :]).astype(jnp.int32)


def draw_owner_map(key, part):
    per_side = SIDE_HI // BLOCK
    quarter = per_side // 4
    per_class = per_side // 2 * (per_side // 2)
    share = per_class // GRIDS
    slot_count = 3 * share
    block_ids = jnp.arange(per_side * per_side, dtype=jnp.int32)
    across = block_ids // per_side
    down_ids = block_ids % per_side
    outer_x = (across < quarter) | (across >= per_side - quarter)
    outer_y = (down_ids < quarter) | (down_ids >= per_side - quarter)
    members = [outer_x & outer_y, outer_y & ~outer_x, outer_x & ~outer_y]
    result = jnp.full(block_ids.shape, -1, jnp.int32)
    for number, member in enumerate(members):
        rank_in = jnp.cumsum(member.astype(jnp.int32)) - 1
        ordering = jax.random.permutation(jax.random.fold_in(key, number + 1), per_class).astype(jnp.int32)
        picked = ordering[jnp.clip(rank_in, 0, per_class - 1)]
        owner_id = picked % GRIDS
        slot_id = number * share + picked // GRIDS
        result = jnp.where(member, owner_id * slot_count + slot_id, result)
    return result.astype(jnp.int32)


def with_ends(drawn, key, low, top_value):
    longest = drawn.shape.index(max(drawn.shape))
    spots = []
    for shift in (0, 1):
        where = [jax.random.randint(jax.random.fold_in(key, axis), (), 0, length) for axis, length in enumerate(drawn.shape)]
        where[longest] = (where[longest] + shift) % drawn.shape[longest]
        spots.append(tuple(where))
    return drawn.at[spots[0]].set(low).at[spots[1]].set(top_value)


def steps_of(key, shape, shards, smallest, high):
    factor_of = 1.0
    for dim, blocks in shards:
        steps = jax.random.uniform(jax.random.fold_in(jax.random.fold_in(key, 6), dim), (blocks,), jnp.float32, smallest / len(shards), high / len(shards))
        factor_of = factor_of * jnp.repeat(jnp.exp(steps), shape[dim] // blocks).reshape((-1,) + (1,) * (len(shape) - 1 - dim))
    return factor_of


def scatter_about(key, dims, spread, most, shards=(), held_as=jnp.bfloat16):
    values = jax.random.normal(key, dims, jnp.float32) * spread
    if len(shards) > 0:
        values = steps_of(key, dims, shards, -0.22, 0.18) * values
    return jnp.clip(values, min=-most, max=most).astype(held_as)


def setup_inputs(seed: int = 0) -> dict:
    streams_of = jax.random.split(jax.random.key(seed), 8)
    field = scatter_about(streams_of[0], (GRIDS, SIDE_HI, SIDE_MID, SIDE_Z), 1.0, 6.0, ((0, 16), (1, 16)))
    levels = draw_levels(jax.random.fold_in(streams_of[7], 71), 0)
    coefficients = with_ends(jax.random.randint(streams_of[2], (GRIDS,), -2, 3), jax.random.fold_in(streams_of[2], 1), -2, 2).astype(jnp.int32)
    failed = with_ends((jax.random.randint(streams_of[3], (GRIDS,), 0, 4) < 1).astype(jnp.int32), jax.random.fold_in(streams_of[3], 1), 0, 1)
    owner_map = draw_owner_map(jax.random.fold_in(streams_of[7], 71), 0)
    velocity = jnp.clip(jax.random.uniform(streams_of[5], (3,), jnp.float32, -1.0, 1.0), -1.0, 1.0)
    diffusivity = jnp.clip(jnp.exp(jax.random.uniform(streams_of[6], (3,), jnp.float32, math.log(0.5), math.log(4.0))), 0.5, 4.0)
    return dict(field=field, levels=levels, coefficients=coefficients, failed=failed, owner_map=owner_map, velocity=velocity, diffusivity=diffusivity)


def signed_modes(positions, length):
    return jnp.where(positions < length // 2, positions, positions - length).astype(jnp.float32)

def dft_tables(length):
    positions = jnp.arange(length, dtype=jnp.int32)
    product = positions[:, None] * positions[None, :] % length
    angles = product.astype(jnp.float32) * (2.0 * math.pi / length)
    return jnp.stack([jnp.cos(angles), -jnp.sin(angles)]).astype(jnp.bfloat16)

def complex_table(length):
    tables = dft_tables(length)
    return jnp.stack([jnp.stack([tables[0], -tables[1]]), jnp.stack([tables[1], tables[0]])])

def apply_factor(spectrum, z_modes, long_modes, mid_modes, swapped, velocity, diffusivity, long_len, mid_len, z_len):
    nu_long = jnp.where(swapped, diffusivity[1], diffusivity[0])
    nu_mid = jnp.where(swapped, diffusivity[0], diffusivity[1])
    speed_long = jnp.where(swapped, velocity[1], velocity[0])
    speed_mid = jnp.where(swapped, velocity[0], velocity[1])
    z_grid = z_modes[:, None, None]
    long_grid = long_modes[None, :, None]
    mid_grid = mid_modes[None, None, :]
    exponent = (diffusivity[2] * z_grid * z_grid + nu_long * long_grid * long_grid + nu_mid * mid_grid * mid_grid) * (-4.0 / (long_len * long_len))
    phases = (velocity[2] * z_grid + speed_long * long_grid + speed_mid * mid_grid) * (-2.0 * math.pi / mid_len)
    magnitude = jnp.exp(exponent) * (1.0 / math.sqrt(long_len * mid_len * z_len))
    factor_re = magnitude * jnp.cos(phases)
    factor_im = magnitude * jnp.sin(phases)
    real_part = spectrum[0] * factor_re - spectrum[1] * factor_im
    imag_part = spectrum[0] * factor_im + spectrum[1] * factor_re
    return jnp.stack([real_part, imag_part])

def block_rows(swapped, owner_map, per_long, per_mid):
    along_long = jnp.arange(per_long, dtype=jnp.int32)[:, None] * jnp.ones((1, per_mid), jnp.int32)
    mid_raw = jnp.arange(per_mid, dtype=jnp.int32)
    mid_global = jnp.where(mid_raw < per_mid // 2, mid_raw, mid_raw + per_long - per_mid)
    along_mid = jnp.ones((per_long, 1), jnp.int32) * mid_global[None, :]
    block_x = jnp.where(swapped, along_mid, along_long)
    block_y = jnp.where(swapped, along_long, along_mid)
    return owner_map[(block_x * per_long + block_y).reshape(-1)]

def to_blocks(shifted, swapped, block_len):
    z_len = shifted.shape[1]
    per_long = shifted.shape[2] // block_len
    per_mid = shifted.shape[3] // block_len
    grouped = shifted.reshape(2, z_len, per_long, block_len, per_mid, block_len).transpose(2, 4, 0, 1, 3, 5)
    turned = jnp.where(swapped, grouped.transpose(0, 1, 2, 3, 5, 4), grouped)
    return turned.reshape(per_long * per_mid, 2, z_len, block_len * block_len)

def transform_grid(samples, swapped, velocity, diffusivity):
    long_len, mid_len, z_len = samples.shape
    highest = lax.Precision.HIGHEST
    along_z = jnp.einsum('abc,pck->pabk', samples.astype(jnp.float32), dft_tables(z_len).astype(jnp.float32), precision=highest).astype(jnp.bfloat16)
    along_mid = jnp.einsum('qabc,pqbd->padc', along_z.astype(jnp.float32), complex_table(mid_len).astype(jnp.float32), precision=highest).astype(jnp.bfloat16)
    spectrum = jnp.einsum('qabc,pqae->pceb', along_mid.astype(jnp.float32), complex_table(long_len).astype(jnp.float32), precision=highest)
    z_modes = signed_modes(jnp.arange(z_len, dtype=jnp.int32), z_len)
    long_modes = signed_modes(jnp.arange(long_len, dtype=jnp.int32), long_len)
    mid_modes = signed_modes(jnp.arange(mid_len, dtype=jnp.int32), mid_len)
    return apply_factor(spectrum, z_modes, long_modes, mid_modes, swapped, velocity, diffusivity, long_len, mid_len, z_len)

def reference(field, levels, coefficients, failed, owner_map, velocity, diffusivity):
    per_long = SIDE_HI // BLOCK
    per_mid = SIDE_MID // BLOCK

    def add_grid(combined, inputs):
        samples, level_row, coefficient, failure = inputs
        swapped = level_row[0] < level_row[1]
        shifted = transform_grid(samples, swapped, velocity, diffusivity)
        blocks = to_blocks(shifted, swapped, BLOCK)
        row_ids = block_rows(swapped, owner_map, per_long, per_mid)
        weight = (coefficient * (1 - failure)).astype(jnp.float32)
        return (combined.at[row_ids].add(weight * blocks), None)
    initial = jnp.zeros((GRIDS * SLOTS, 2, SIDE_Z, BLOCK * BLOCK), jnp.float32)
    combined, _ = lax.scan(add_grid, initial, (field, levels, coefficients, failed))
    return combined
```

```python
import functools
import math

import jax
import jax.numpy as jnp
import ml_dtypes
import numpy as np
from jax import lax
from jax.sharding import PartitionSpec as P

BF16 = ml_dtypes.bfloat16


def dft_table(length):
    positions = np.arange(length, dtype=np.int64)
    angles = (positions[:, None] * positions[None, :] % length) * (2.0 * math.pi / length)
    return np.cos(angles).astype(BF16).astype(np.float32), (-np.sin(angles)).astype(BF16).astype(np.float32)


def slot_positions(g):
    return [2 * g, 32 if g == 0 else 64 - 2 * g, 2 * g + 1, 63 - 2 * g]


@functools.cache
def mid_table():
    cos, sin = dft_table(256)
    rows = np.zeros((16, 2, 4, 2, 256), np.float32)
    for g in range(16):
        for grp in range(2):
            for i, n in enumerate(slot_positions(g)):
                m = n + 64 * grp
                rows[g, grp, i, 0] = cos[m]
                rows[g, grp, i, 1] = sin[m]
    rows[0, 0, 0, 1] = cos[128]
    return rows.reshape(256, 256).astype(BF16)


@functools.cache
def z_tables():
    cos, sin = dft_table(128)
    c = cos.reshape(16, 8, 128).transpose(2, 0, 1)
    s = sin.reshape(16, 8, 128).transpose(2, 0, 1)
    e = (c, s)
    ie = (-s, c)
    out = np.zeros((3, 2, 2, 128, 16, 2, 2, 2, 8), np.float32)

    def put(variant, i2, ab, sign, slot, pair, scale):
        for q in range(2):
            out[variant, i2, ab, :, :, sign, slot, q, :] = scale * pair[q]

    for variant in range(3):
        for i2 in range(2):
            if variant == 1 and i2 == 0:
                put(1, 0, 0, 0, 0, e, 1.0)
                put(1, 0, 1, 1, 0, e, 1.0)
                continue
            back = 1 - i2 if variant == 0 else i2
            put(variant, i2, 0, 0, i2, e, 1.0)
            put(variant, i2, 1, 0, i2, ie, 1.0)
            put(variant, i2, 0, 1, back, e, 1.0)
            put(variant, i2, 1, 1, back, ie, -1.0)
    return out.reshape(3, 512, 1024).astype(BF16)


@functools.cache
def long_table():
    cos, sin = dft_table(512)
    return np.concatenate([cos, sin], axis=1).astype(BF16)


def owner_codes(owner_map):
    ids = jnp.arange(64, dtype=jnp.int32)
    bx, by = ids // 8, ids % 8
    in_x, in_y = (bx >= 2) & (bx < 6), (by >= 2) & (by < 6)
    kind = jnp.where(in_x, 1, jnp.where(in_y, 2, 0))
    key = jnp.where(owner_map >= 0, (owner_map // 3) * 3 + kind, -1)
    match = key[None, :] == jnp.arange(48, dtype=jnp.int32)[:, None]
    return jnp.sum(jnp.where(match, (ids * 4 + owner_map % 3)[None, :], 0), axis=1)


def body(field, levels, coefficients, failed, owner_map, velocity, diffusivity):
    g = lax.axis_index("grid")
    p = lax.axis_index("pencil")
    kind = (levels[0, 0] < levels[0, 1]).astype(jnp.int32)
    weight = (coefficients[0] * (1 - failed[0])).astype(jnp.float32)
    v = jnp.einsum("rm,amz->arz", jnp.asarray(mid_table()), field[0], preferred_element_type=jnp.float32)
    v = (v * weight).astype(jnp.bfloat16)
    zero = jnp.zeros_like(v)
    both = jnp.stack([jnp.where(kind == 0, v, zero), jnp.where(kind == 1, v, zero)])
    both = both.reshape(2, 32, 16, 16, 128)
    s = lax.psum_scatter(both, "grid", scatter_dimension=2, tiled=False)
    s = s.reshape(2, 32, 2, 2, 512)
    w = jnp.asarray(z_tables())
    first = g == 0
    wa = jnp.where(first, w[1], w[0])
    wb = jnp.where(first, w[2], w[0])
    f32 = jnp.float32
    u0a = jnp.einsum("kaz,zn->kan", s[:, :, 0, 0], wa, preferred_element_type=f32)
    u0b = jnp.einsum("kaz,zn->kan", s[:, :, 1, 0], wb, preferred_element_type=f32)
    u1 = jnp.einsum("kacz,zn->kacn", s[:, :, :, 1], w[0], preferred_element_type=f32)
    lane = jnp.arange(1024) % 64
    swap = first & (lane >= 32) & (lane < 48)
    u0 = jnp.stack([jnp.where(swap, u0b, u0a), jnp.where(swap, u0a, u0b)], axis=2)
    u = jnp.stack([u0, u1], axis=3).astype(jnp.bfloat16)
    chunk = u.reshape(2, 32, 2, 2, 16, 64).transpose(4, 0, 2, 1, 3, 5).reshape(16, 4, 32, 128)
    r = lax.all_to_all(chunk, "pencil", split_axis=0, concat_axis=0, tiled=True)
    table = jnp.asarray(long_table()).reshape(16, 32, 1024)
    res = jnp.einsum("pkal,pan->kln", r, table, preferred_element_type=f32)
    res = res.reshape(2, 2, 2, 2, 2, 2, 8, 2, 512)
    re = res[:, :, :, :, :, 0, :, 0] - res[:, :, :, :, :, 1, :, 1]
    im = res[:, :, :, :, :, 1, :, 0] + res[:, :, :, :, :, 0, :, 1]
    longs = jnp.arange(512, dtype=jnp.int32)
    k_long = jnp.where(longs < 256, longs, longs - 512).astype(f32)
    n0 = jnp.array([0, 64, 1, 63]) + g * jnp.array([2, -2, 2, -2])
    n = jnp.where((g == 0) & (jnp.arange(4) == 1), 32, n0).reshape(2, 2)
    base = jnp.array([[0, -64], [64, -128]])
    k_mid = (n[None, :, None, :] + base[:, None, :, None]).astype(f32)
    zs = p * 8 + jnp.arange(8, dtype=jnp.int32)
    k_z = jnp.where(zs < 64, zs, zs - 128).astype(f32)
    shape = (2, 2, 2, 2, 2, 8, 512)
    kl = jnp.broadcast_to(k_long, shape)
    km = jnp.broadcast_to(k_mid[None, :, :, :, :, None, None], shape)
    kz = jnp.broadcast_to(k_z[:, None], shape)
    is0 = (jnp.arange(2) == 0).reshape(2, 1, 1, 1, 1, 1, 1)
    kx, ky = jnp.where(is0, kl, km), jnp.where(is0, km, kl)
    expo = (diffusivity[0] * kx * kx + diffusivity[1] * ky * ky + diffusivity[2] * kz * kz) * (-4.0 / 512**2)
    phase = (velocity[0] * kx + velocity[1] * ky + velocity[2] * kz) * (-2.0 * math.pi / 256)
    mag = jnp.exp(expo) * (1.0 / 4096)
    fr, fi = mag * jnp.cos(phase), mag * jnp.sin(phase)
    f = jnp.stack([re * fr - im * fi, re * fi + im * fr], axis=5).astype(jnp.bfloat16)
    f = f.reshape(2, 2, 2, 2, 2, 2, 8, 8, 64).transpose(0, 1, 3, 7, 2, 4, 5, 6, 8).reshape(2, 32, 4, 2, 8, 64)
    codes = owner_codes(owner_map).reshape(16, 3)
    blk = codes // 4
    bx, by = blk // 8, blk % 8

    def index(lb, gb):
        sign = gb // 4
        grp = (gb % 2) ^ sign
        return (grp * 2 + sign) * 8 + lb

    i0 = index(bx[:, :2], by[:, :2])
    i1 = index(jnp.stack([by[:, 0], by[:, 2]], 1), jnp.stack([bx[:, 0], bx[:, 2]], 1))
    out = jnp.stack([f[0][i0], f[1][i1]], axis=1)
    rb = lax.all_to_all(out, "grid", split_axis=0, concat_axis=0, tiled=True)
    order = np.zeros(64, np.int32)
    for gg in range(16):
        for i, nn in enumerate(slot_positions(gg)):
            order[nn] = gg * 4 + i
    rb = rb.astype(f32).transpose(1, 2, 4, 5, 0, 3, 6).reshape(2, 2, 2, 8, 64, 64)[:, :, :, :, order]
    k0 = rb[0].transpose(0, 1, 2, 4, 3)
    k1 = rb[1]
    classes = jnp.stack([k0[0] + k1[0], k0[1], k1[1]]).reshape(3, 2, 8, 4096)
    slots = codes[g] % 4
    which = jnp.sum(jnp.where(slots[None, :] == jnp.arange(3)[:, None], jnp.arange(3)[None, :], 0), axis=1)
    return classes[which]


def solution(mesh):
    placed = (P("grid", "pencil", None, None), P("grid", None), P("grid"), P("grid"), P(), P(), P())
    return jax.shard_map(
        body, mesh=mesh, in_specs=placed, out_specs=P("grid", None, "pencil", None), check_vma=False
    )
```

```python
import functools
import math

import jax
import jax.numpy as jnp
import ml_dtypes
import numpy as np
from jax import lax
from jax.experimental import pallas as pl
from jax.experimental.pallas import tpu as pltpu
from jax.sharding import PartitionSpec as P

BF16 = ml_dtypes.bfloat16
F32 = jnp.float32
MESH = pl.DeviceIdType.MESH


def dft_table(length):
    positions = np.arange(length, dtype=np.int64)
    angles = (positions[:, None] * positions[None, :] % length) * (2.0 * math.pi / length)
    return np.cos(angles).astype(BF16).astype(np.float32), (-np.sin(angles)).astype(BF16).astype(np.float32)


def slot_positions(g):
    return [2 * g, 32 if g == 0 else 64 - 2 * g, 2 * g + 1, 63 - 2 * g]


@functools.cache
def mid_table():
    cos, sin = dft_table(256)
    rows = np.zeros((16, 2, 4, 2, 256), np.float32)
    for g in range(16):
        for grp in range(2):
            for i, n in enumerate(slot_positions(g)):
                rows[g, grp, i, 0] = cos[n + 64 * grp]
                rows[g, grp, i, 1] = sin[n + 64 * grp]
    rows[0, 0, 0, 1] = cos[128]
    return rows.reshape(256, 256).astype(BF16)


@functools.cache
def z_bases():
    cos, sin = dft_table(128)
    c = cos.reshape(16, 8, 128).transpose(2, 0, 1)
    s = sin.reshape(16, 8, 128).transpose(2, 0, 1)
    both = np.stack([np.stack([c, s], 2), np.stack([-s, c], 2)])
    full = np.broadcast_to(both[:, :, :, None], (2, 128, 16, 4, 2, 8))
    return full.reshape(2, 128, 1024).astype(BF16)


@functools.cache
def z_masks():
    out = np.zeros((3, 2, 2, 2, 16, 2, 2, 16), np.float32)

    def put(variant, i2, ab, sign, slot, which, scale):
        out[variant, i2, ab, which, :, sign, slot] = scale

    for variant in range(3):
        for i2 in range(2):
            if variant == 1 and i2 == 0:
                put(1, 0, 0, 0, 0, 0, 1.0)
                put(1, 0, 1, 1, 0, 0, 1.0)
                continue
            back = 1 - i2 if variant == 0 else i2
            put(variant, i2, 0, 0, i2, 0, 1.0)
            put(variant, i2, 1, 0, i2, 1, 1.0)
            put(variant, i2, 0, 1, back, 0, 1.0)
            put(variant, i2, 1, 1, back, 1, -1.0)
    return out.reshape(24, 1, 1024)


@functools.cache
def long_table():
    cos, sin = dft_table(512)
    return np.concatenate([cos, sin], axis=1).astype(BF16)


@functools.cache
def order_table():
    out = np.zeros((64, 128), np.float32)
    for g in range(16):
        for i, n in enumerate(slot_positions(g)):
            out[g * 4 + i, n] = 1.0
            out[g * 4 + i, n + 64] = 1.0
    return out.astype(BF16)


def owner_codes(owner_map):
    ids = jnp.arange(64, dtype=jnp.int32)
    bx, by = ids // 8, ids % 8
    in_x, in_y = (bx >= 2) & (bx < 6), (by >= 2) & (by < 6)
    kind = jnp.where(in_x, 1, jnp.where(in_y, 2, 0))
    key = jnp.where(owner_map >= 0, (owner_map // 3) * 3 + kind, -1)
    match = key[None, :] == jnp.arange(48, dtype=jnp.int32)[:, None]
    return jnp.sum(jnp.where(match, (ids * 4 + owner_map % 3)[None, :], 0), axis=1, dtype=jnp.int32)


PLUS_D = (4, 3, 3, 2, 2, 1, 1)
PLUS_H = (0, 1, 0, 1, 0, 1, 0)


def transform_kernel(
    levels, coefficients, failed, codes, velocity, diffusivity, field, mid_tab, base_tab, masks, long_tab,
    landing,
    fbuf, tbuf, ebuf, tlbuf, wbuf, v, xr, xk, sb, rz, sf, lhs0, lhs1, chunk, rows, ff, sb2, flong, frow,
    load_sem, xs_sem, xr_sem, zs_sem, zr_sem, ps_sem, pr_sem, gs_sem, gr_sem,
):
    g = lax.axis_index("grid")
    p = lax.axis_index("pencil")
    zc, core = g // 2, g % 2
    py, px = p // 4, p % 4

    loads = [
        pltpu.make_async_copy(mid_tab, tbuf, load_sem.at[0]),
        pltpu.make_async_copy(field.at[0, pl.ds(0, 16)], fbuf.at[pl.ds(0, 16)], load_sem.at[1]),
        pltpu.make_async_copy(field.at[0, pl.ds(16, 16)], fbuf.at[pl.ds(16, 16)], load_sem.at[2]),
        pltpu.make_async_copy(base_tab, ebuf, load_sem.at[3]),
        pltpu.make_async_copy(long_tab, tlbuf, load_sem.at[4]),
    ]
    for load in loads:
        load.start()

    barrier = pltpu.get_barrier_semaphore()
    for s in range(1, 16):
        og = 2 * lax.rem(zc + s // 2, 8) + lax.rem(core + s % 2, 2)
        pl.semaphore_signal(barrier, inc=1, device_id=(og, p), device_id_type=MESH)
        op = 4 * lax.rem(py + s // 4, 4) + lax.rem(px + s % 4, 4)
        pl.semaphore_signal(barrier, inc=1, device_id=(g, op), device_id_type=MESH)

    kind = jnp.where(levels[0, 0] < levels[0, 1], 1.0, 0.0).astype(F32)
    weight = (coefficients[0] * (1 - failed[0])).astype(F32)
    loads[0].wait()

    def mid_step(k, carry):
        pair = jnp.concatenate([fbuf[2 * k], fbuf[2 * k + 1]], axis=1)
        y = jnp.dot(tbuf[...], pair, preferred_element_type=F32) * weight
        yb = y.astype(jnp.bfloat16)
        v[:, pl.ds(2 * k, 1)] = yb[:, :128].reshape(16, 1, 16, 128)
        v[:, pl.ds(2 * k + 1, 1)] = yb[:, 128:].reshape(16, 1, 16, 128)
        return carry

    loads[1].wait()
    lax.fori_loop(0, 8, mid_step, 0)
    loads[2].wait()
    lax.fori_loop(8, 16, mid_step, 0)

    xk[0] = jnp.full((16, 128), kind, F32)
    pl.semaphore_wait(barrier, 30)

    mate = (g + 1 - 2 * core, p)
    kind_copy = pltpu.make_async_remote_copy(
        xk.at[0], xk.at[1], xs_sem.at[16], xr_sem.at[16], device_id=mate, device_id_type=MESH
    )
    kind_copy.start()
    swaps = {}
    order = [(4, 0), (4, 1), (3, 1), (5, 0), (3, 0), (5, 1), (2, 1), (6, 0), (2, 0), (6, 1)]
    order += [(1, 1), (7, 0), (1, 0), (7, 1), (0, 0), (0, 1)]
    for d, h in order:
        z = lax.rem(zc + d, 8)
        swaps[d, h] = pltpu.make_async_remote_copy(
            v.at[2 * z + 1 - core, pl.ds(16 * h, 16)],
            xr.at[z, pl.ds(16 * h, 16)],
            xs_sem.at[2 * d + h],
            xr_sem.at[2 * d + h],
            device_id=mate,
            device_id_type=MESH,
        )
        swaps[d, h].start()
    kind_copy.wait_recv()
    other = xk[1][None]
    mine = kind

    def own_sum(z, at, k):
        me = v[2 * z + core, pl.ds(at, 4)].astype(F32)
        mate_part = xr[z, pl.ds(at, 4)].astype(F32)
        if k == 0:
            return me * (1.0 - mine) + mate_part * (1.0 - other)
        return me * mine + mate_part * other

    hops = {}
    for n in range(7):
        for way in range(2):
            d = PLUS_D[n] if way == 0 else 8 - PLUS_D[n]
            h = PLUS_H[n] if way == 0 else 1 - PLUS_H[n]
            z = lax.rem(zc + d, 8)
            swaps[d, h].wait_recv()
            if n >= 2:
                hops[way, n - 2].wait_recv()

            def add_step(a, carry, n=n, way=way, h=h, z=z):
                for k in range(2):
                    total = own_sum(z, 16 * h + 4 * a, k)
                    if n >= 2:
                        total = total + rz[way, n - 2, k, pl.ds(4 * a, 4)].astype(F32)
                    sb[way, n, k, pl.ds(4 * a, 4)] = total.astype(jnp.bfloat16)
                return carry

            lax.fori_loop(0, 4, add_step, 0)
            to = lax.rem(zc + (1 if way == 0 else 7), 8)
            hops[way, n] = pltpu.make_async_remote_copy(
                sb.at[way, n],
                rz.at[way, n],
                zs_sem.at[way, n],
                zr_sem.at[way, n],
                device_id=(2 * to + core, p),
                device_id_type=MESH,
            )
            hops[way, n].start()

    loads[3].wait()
    first = jnp.where(g == 0, 1, 0)
    for variant in range(3):
        var = variant * first
        for blk in range(4):

            def table_step(c, carry, variant=variant, blk=blk, var=var):
                at = pl.ds(16 * c, 16)
                me = masks[8 * var + 2 * blk]
                mi = masks[8 * var + 2 * blk + 1]
                val = ebuf[0, at].astype(F32) * me + ebuf[1, at].astype(F32) * mi
                wbuf[variant, pl.ds(128 * blk + 16 * c, 16)] = val.astype(jnp.bfloat16)
                return carry

            lax.fori_loop(0, 8, table_step, 0)

    lanes = lax.broadcasted_iota(jnp.int32, (8, 512), 1)
    k_long = jnp.where(lanes < 256, lanes, lanes - 512).astype(F32)
    for k in range(2):
        mag = jnp.exp(diffusivity[k] * k_long * k_long * (-4.0 / 512**2))
        ph = velocity[k] * k_long * (-2.0 * math.pi / 256)
        flong[k, 0] = mag * jnp.cos(ph)
        flong[k, 1] = mag * jnp.sin(ph)

    def row_step(k, carry):
        r = lax.broadcasted_iota(jnp.int32, (128, 128), 0)
        i2, sign = (r >> 3) & 1, (r >> 4) & 1
        pair, grp = (r >> 5) & 1, (r >> 6) & 1
        pos = jnp.where(i2 == 0, 2 * g + pair, jnp.where((pair == 0) & (g == 0), 32, 64 - 2 * g - pair))
        base = jnp.where(grp == 0, -64 * sign, 64 - 192 * sign)
        k_mid = (pos + base).astype(F32)
        zi = 8 * p + (r & 7)
        k_z = jnp.where(zi < 64, zi, zi - 128).astype(F32)
        d_mid = diffusivity[1 - k]
        v_mid = velocity[1 - k]
        mag = jnp.exp((d_mid * k_mid * k_mid + diffusivity[2] * k_z * k_z) * (-4.0 / 512**2)) * (1.0 / 4096)
        ph = (v_mid * k_mid + velocity[2] * k_z) * (-2.0 * math.pi / 256)
        frow[k, 0] = mag * jnp.cos(ph)
        frow[k, 1] = mag * jnp.sin(ph)
        return carry

    for k in range(2):
        row_step(k, 0)

    for h in range(2):
        swaps[0, h].wait_recv()
        a_way, b_way = (6, 5) if h == 0 else (5, 6)
        hops[0, a_way].wait_recv()
        hops[1, b_way].wait_recv()

        def last_step(a, carry, h=h, a_way=a_way, b_way=b_way):
            for k in range(2):
                total = own_sum(zc, 16 * h + 4 * a, k)
                total = total + rz[0, a_way, k, pl.ds(4 * a, 4)].astype(F32)
                total = total + rz[1, b_way, k, pl.ds(4 * a, 4)].astype(F32)
                sf[k, pl.ds(256 * h + 64 * a, 64)] = total.reshape(64, 128)
            return carry

        lax.fori_loop(0, 4, last_step, 0)

    for k in range(2):
        for grp in range(2):
            for pair in range(2):
                for e in range(4):
                    j = grp * 8 + pair * 4 + e
                    part = sf[k, pl.ds(j, 32, stride=16)].astype(jnp.bfloat16)
                    if pair == 0:
                        lhs0[grp, pl.ds(32 * k, 32), pl.ds(128 * e, 128)] = part
                    else:
                        lhs1[pl.ds(64 * k + 32 * grp, 32), pl.ds(128 * e, 128)] = part
    lane64 = lax.broadcasted_iota(jnp.int32, (64, 128), 1)
    l64 = lane64 % 64
    low = lane64 < 64
    swap = (l64 >= 32) & (l64 < 48) & (g == 0)
    low32 = low[:32]
    for t in range(8):
        cols = pl.ds(128 * t, 128)
        ua = jnp.dot(lhs0[0], wbuf[1, :, cols], preferred_element_type=F32)
        ub = jnp.dot(lhs0[1], wbuf[2, :, cols], preferred_element_type=F32)
        u1 = jnp.dot(lhs1[...], wbuf[0, :, cols], preferred_element_type=F32)
        u0 = (jnp.where(swap, ub, ua), jnp.where(swap, ua, ub))
        u0r = (pltpu.roll(u0[0], 64, 1), pltpu.roll(u0[1], 64, 1))
        u1r = pltpu.roll(u1, 64, 1)
        for k in range(2):
            for grp in range(2):
                at = slice(64 * k + 32 * grp, 64 * k + 32 * grp + 32)
                a0, a0r = u0[grp][32 * k : 32 * k + 32], u0r[grp][32 * k : 32 * k + 32]
                chunk[2 * t, 2 * k + grp] = jnp.where(low32, a0, u1r[at]).astype(jnp.bfloat16)
                chunk[2 * t + 1, 2 * k + grp] = jnp.where(low32, a0r, u1[at]).astype(jnp.bfloat16)

    outs = []
    for s in (10, 11, 14, 9, 6, 15, 13, 7, 5, 8, 2, 12, 4, 3, 1):
        op = 4 * lax.rem(py + s // 4, 4) + lax.rem(px + s % 4, 4)
        copy = pltpu.make_async_remote_copy(
            chunk.at[op], rows.at[p], ps_sem.at[s], pr_sem.at[s], device_id=(g, op), device_id_type=MESH
        )
        copy.start()
        outs.append(copy)
    rows[pl.ds(p, 1)] = chunk[pl.ds(p, 1)]
    loads[4].wait()
    for copy in outs:
        copy.wait_recv()

    for kg in range(4):
        k = kg // 2
        line = rows[:, kg].reshape(512, 128)
        turned = line.T
        for t in range(4):
            col_c = tlbuf[:, pl.ds(128 * t, 128)]
            col_s = tlbuf[:, pl.ds(512 + 128 * t, 128)]
            both = jnp.dot(turned, jnp.concatenate([col_c, col_s], axis=1), preferred_element_type=F32)
            c = both[:, :128].reshape(8, 2, 8, 128)
            sn = both[:, 128:].reshape(8, 2, 8, 128)
            re = c[:, 0] - sn[:, 1]
            im = c[:, 1] + sn[:, 0]
            rr = frow[k, 0, pl.ds(64 * (kg % 2), 64)].reshape(8, 8, 128)
            ri = frow[k, 1, pl.ds(64 * (kg % 2), 64)].reshape(8, 8, 128)
            lr = flong[k, 0, :, pl.ds(128 * t, 128)][None]
            li = flong[k, 1, :, pl.ds(128 * t, 128)][None]
            er = rr * lr - ri * li
            ei = rr * li + ri * lr
            out_re = re * er - im * ei
            out_im = re * ei + im * er
            full = jnp.stack([out_re, out_im], axis=1).reshape(2, 2, 2, 16, 128)
            spun = pltpu.roll(full.reshape(128, 128), 64, 1).reshape(2, 2, 2, 16, 128)
            for sign in range(2):
                at = ((kg * 2 + 0) * 4 + t) * 2 + sign
                ff[at] = full[:, sign].reshape(64, 128).astype(jnp.bfloat16)
                ff[at + 8] = spun[:, sign].reshape(64, 128).astype(jnp.bfloat16)

    def piece(k, lb, gb, high):
        sign = gb >> 2
        grp = (gb & 1) ^ sign
        rot = (lb & 1) if high == 0 else 1 - (lb & 1)
        at = (((2 * k + grp) * 2 + rot) * 4 + (lb >> 1)) * 2 + sign
        return ff[at].astype(F32)

    finals = []
    for s in (8, 9, 7, 6, 10, 11, 5, 4, 12, 13, 3, 2, 14, 15, 1, 0):
        og = 2 * lax.rem(zc + s // 2, 8) + lax.rem(core + s % 2, 2)
        ca, cb, cc = (codes[3 * og + c] >> 2 for c in range(3))
        ax, ay = ca >> 3, ca & 7
        bx, by = cb >> 3, cb & 7
        cx, cy = cc >> 3, cc & 7
        sb2[s, 0] = jnp.where(low, piece(0, ax, ay, 0), piece(0, bx, by, 1)).astype(jnp.bfloat16)
        sb2[s, 1] = jnp.where(low, piece(1, ay, ax, 0), piece(1, cy, cx, 1)).astype(jnp.bfloat16)
        if s:
            copy = pltpu.make_async_remote_copy(
                sb2.at[s], landing.at[g], gs_sem.at[s], gr_sem.at[s], device_id=(og, p), device_id_type=MESH
            )
            copy.start()
            finals.append(copy)
        else:
            own = pltpu.make_async_copy(sb2.at[0], landing.at[g], gs_sem.at[0])
            own.start()
    own.wait()
    for copy in finals:
        copy.wait()
    for copy in outs:
        copy.wait_send()
    for copy in hops.values():
        copy.wait_send()
    for copy in swaps.values():
        copy.wait_send()
    kind_copy.wait_send()


def place_kernel(codes, landed, order, out, f0, d0, k0):
    g = lax.axis_index("grid")
    slot = [codes[3 * g + c] & 3 for c in range(3)]
    for gg in range(16):
        f0[pl.ds(64 * gg, 64)] = landed[gg, 0].astype(F32)
    low32 = lax.broadcasted_iota(jnp.int32, (32, 128), 1) < 64
    low8 = low32[:8]
    for q in range(2):
        for z in range(8):
            rows = f0[pl.ds(8 * q + z, 64, stride=16)].astype(jnp.bfloat16)
            buf = z % 2
            d0[buf] = jnp.dot(rows.T, order[...], preferred_element_type=F32)
            for c in range(2):
                even = d0[buf, pl.ds(64 * c, 32, stride=2)]
                odd = d0[buf, pl.ds(64 * c + 1, 32, stride=2)]
                k0[c, q, pl.ds(z, 32, stride=8)] = jnp.where(low32, even, odd)
    for x2 in range(32):
        ge, ie = (x2, 0) if x2 < 16 else ((0, 1) if x2 == 16 else (32 - x2, 1))
        go, io = (x2, 2) if x2 < 16 else (31 - x2, 3)
        even = landed[ge, 1, pl.ds(16 * ie, 16)].astype(F32)
        odd = landed[go, 1, pl.ds(16 * io, 16)].astype(F32)
        for q in range(2):
            e, o = even[8 * q : 8 * q + 8], odd[8 * q : 8 * q + 8]
            first = jnp.where(low8, e, pltpu.roll(o, 64, 1))
            third = jnp.where(low8, pltpu.roll(e, 64, 1), o)
            at = pl.ds(8 * x2, 8)
            cols = pl.ds(128 * x2, 128)
            out[slot[0], q, :, cols] = first + k0[0, q, at]
            out[slot[1], q, :, cols] = k0[1, q, at]
            out[slot[2], q, :, cols] = third


def body(field, levels, coefficients, failed, owner_map, velocity, diffusivity):
    codes = owner_codes(owner_map)
    smem = pl.BlockSpec(memory_space=pltpu.SMEM)
    vmem = pl.BlockSpec(memory_space=pltpu.VMEM)
    anyspace = pl.BlockSpec(memory_space=pl.ANY)
    bf = jnp.bfloat16
    dma = pltpu.SemaphoreType.DMA
    landed = pl.pallas_call(
        transform_kernel,
        out_shape=jax.ShapeDtypeStruct((16, 2, 64, 128), bf),
        in_specs=[smem] * 6 + [anyspace] * 3 + [vmem] + [anyspace],
        out_specs=anyspace,
        scratch_shapes=[
            pltpu.VMEM((32, 256, 128), bf),
            pltpu.VMEM((256, 256), bf),
            pltpu.VMEM((2, 128, 1024), bf),
            pltpu.VMEM((512, 1024), bf),
            pltpu.VMEM((3, 512, 1024), bf),
            pltpu.VMEM((16, 32, 16, 128), bf),
            pltpu.VMEM((8, 32, 16, 128), bf),
            pltpu.VMEM((2, 16, 128), F32),
            pltpu.VMEM((2, 7, 2, 16, 16, 128), bf),
            pltpu.VMEM((2, 7, 2, 16, 16, 128), bf),
            pltpu.VMEM((2, 512, 128), F32),
            pltpu.VMEM((2, 64, 512), bf),
            pltpu.VMEM((128, 512), bf),
            pltpu.VMEM((16, 4, 32, 128), bf),
            pltpu.VMEM((16, 4, 32, 128), bf),
            pltpu.VMEM((64, 64, 128), bf),
            pltpu.VMEM((16, 2, 64, 128), bf),
            pltpu.VMEM((2, 2, 8, 512), F32),
            pltpu.VMEM((2, 2, 128, 128), F32),
            dma((5,)), dma((17,)), dma((17,)), dma((2, 7)), dma((2, 7)),
            dma((16,)), dma((16,)), dma((16,)), dma((16,)),
        ],
        compiler_params=pltpu.CompilerParams(
            collective_id=0, has_side_effects=True, vmem_limit_bytes=56 * 2**20
        ),
        name="transform",
    )(
        levels, coefficients, failed, codes, velocity, diffusivity, field,
        jnp.asarray(mid_table()), jnp.asarray(z_bases()), jnp.asarray(z_masks()), jnp.asarray(long_table()),
    )
    return pl.pallas_call(
        place_kernel,
        out_shape=jax.ShapeDtypeStruct((3, 2, 8, 4096), F32),
        in_specs=[smem, vmem, vmem],
        out_specs=vmem,
        scratch_shapes=[
            pltpu.VMEM((1024, 128), F32),
            pltpu.VMEM((2, 128, 128), F32),
            pltpu.VMEM((2, 2, 256, 128), F32),
        ],
        compiler_params=pltpu.CompilerParams(vmem_limit_bytes=32 * 2**20),
        name="place",
    )(codes, landed, jnp.asarray(order_table()))


def solution(mesh):
    placed = (P("grid", "pencil", None, None), P("grid", None), P("grid"), P("grid"), P(), P(), P())
    return jax.shard_map(
        body, mesh=mesh, in_specs=placed, out_specs=P("grid", None, "pencil", None), check_vma=False
    )
```

```python
import functools
import math

import jax
import jax.numpy as jnp
import ml_dtypes
import numpy as np
from jax import lax
from jax.experimental import pallas as pl
from jax.experimental.pallas import tpu as pltpu
from jax.sharding import PartitionSpec as P

BF16 = ml_dtypes.bfloat16
F32 = jnp.float32
MESH = pl.DeviceIdType.MESH


def dft_table(length):
    positions = np.arange(length, dtype=np.int64)
    angles = (positions[:, None] * positions[None, :] % length) * (2.0 * math.pi / length)
    return np.cos(angles).astype(BF16).astype(np.float32), (-np.sin(angles)).astype(BF16).astype(np.float32)


def slot_positions(g):
    return [2 * g, 32 if g == 0 else 64 - 2 * g, 2 * g + 1, 63 - 2 * g]


@functools.cache
def mid_table():
    cos, sin = dft_table(256)
    rows = np.zeros((16, 2, 4, 2, 256), np.float32)
    for g in range(16):
        for grp in range(2):
            for i, n in enumerate(slot_positions(g)):
                rows[g, grp, i, 0] = cos[n + 64 * grp]
                rows[g, grp, i, 1] = sin[n + 64 * grp]
    rows[0, 0, 0, 1] = cos[128]
    return rows.reshape(256, 256).astype(BF16)


@functools.cache
def z_bases():
    cos, sin = dft_table(128)
    c = cos.reshape(16, 8, 128).transpose(2, 0, 1)
    s = sin.reshape(16, 8, 128).transpose(2, 0, 1)
    both = np.stack([np.stack([c, s], 2), np.stack([-s, c], 2)])
    full = np.broadcast_to(both[:, :, :, None], (2, 128, 16, 4, 2, 8))
    return full.reshape(2, 128, 1024).astype(BF16)


@functools.cache
def z_masks():
    out = np.zeros((3, 2, 2, 2, 16, 2, 2, 16), np.float32)

    def put(variant, i2, ab, sign, slot, which, scale):
        out[variant, i2, ab, which, :, sign, slot] = scale

    for variant in range(3):
        for i2 in range(2):
            if variant == 1 and i2 == 0:
                put(1, 0, 0, 0, 0, 0, 1.0)
                put(1, 0, 1, 1, 0, 0, 1.0)
                continue
            back = 1 - i2 if variant == 0 else i2
            put(variant, i2, 0, 0, i2, 0, 1.0)
            put(variant, i2, 1, 0, i2, 1, 1.0)
            put(variant, i2, 0, 1, back, 0, 1.0)
            put(variant, i2, 1, 1, back, 1, -1.0)
    return out.reshape(24, 1, 1024)


@functools.cache
def long_table():
    cos, sin = dft_table(512)
    return np.concatenate([cos, sin], axis=1).astype(BF16)


@functools.cache
def order_table():
    out = np.zeros((64, 128), np.float32)
    for g in range(16):
        for i, n in enumerate(slot_positions(g)):
            out[g * 4 + i, n] = 1.0
            out[g * 4 + i, n + 64] = 1.0
    return out.astype(BF16)


PLUS_D = (4, 3, 3, 2, 2, 1, 1)
PLUS_H = (0, 1, 0, 1, 0, 1, 0)
CLASSES = (
    tuple(8 * x + y for x in (0, 1, 6, 7) for y in (0, 1, 6, 7)),
    tuple(8 * x + y for x in (2, 3, 4, 5) for y in (0, 1, 6, 7)),
    tuple(8 * x + y for x in (0, 1, 6, 7) for y in (2, 3, 4, 5)),
)


def block_code(owner_map, owner, c):
    total = 0
    for b in CLASSES[c]:
        r = owner_map[b] - 3 * owner
        total = total + jnp.where((r >= 0) & (r < 3), 4 * b + r, 0)
    return total & 255


def transform_kernel(
    levels, coefficients, failed, owner_map, velocity, diffusivity, field, mid_tab, base_tab, mask_tab, long_tab,
    landing,
    fbuf, tbuf, ebuf, masks, tlbuf, wbuf, v, xr, xk, sb, rz, sf, lhs0, lhs1, chunk, rows, ff, sb2, flong, frow, codes,
    load_sem, xs_sem, xr_sem, zs_sem, zr_sem, ps_sem, pr_sem, gs_sem, gr_sem,
):
    g = lax.axis_index("grid")
    p = lax.axis_index("pencil")
    zc, core = g // 2, g % 2
    py, px = p // 4, p % 4

    loads = [
        pltpu.make_async_copy(mid_tab, tbuf, load_sem.at[0]),
        pltpu.make_async_copy(field.at[0, pl.ds(0, 16)], fbuf.at[pl.ds(0, 16)], load_sem.at[1]),
        pltpu.make_async_copy(field.at[0, pl.ds(16, 16)], fbuf.at[pl.ds(16, 16)], load_sem.at[2]),
        pltpu.make_async_copy(base_tab, ebuf, load_sem.at[3]),
        pltpu.make_async_copy(mask_tab, masks, load_sem.at[4]),
        pltpu.make_async_copy(long_tab, tlbuf, load_sem.at[5]),
    ]
    for load in loads:
        load.start()

    barrier = pltpu.get_barrier_semaphore()
    for s in (8, 9, 6, 7, 10, 11, 4, 5, 12, 13, 2, 3, 14, 15, 1):
        og = 2 * lax.rem(zc + s // 2, 8) + lax.rem(core + s % 2, 2)
        pl.semaphore_signal(barrier, inc=1, device_id=(og, p), device_id_type=MESH)
    for s in range(1, 16):
        op = 4 * lax.rem(py + s // 4, 4) + lax.rem(px + s % 4, 4)
        pl.semaphore_signal(barrier, inc=1, device_id=(g, op), device_id_type=MESH)

    kind = jnp.where(levels[0, 0] < levels[0, 1], 1.0, 0.0).astype(F32)
    weight = (coefficients[0] * (1 - failed[0])).astype(F32)
    loads[0].wait()

    def mid_step(k, carry):
        pair = jnp.concatenate([fbuf[2 * k], fbuf[2 * k + 1]], axis=1)
        y = jnp.dot(tbuf[...], pair, preferred_element_type=F32) * weight
        yb = y.astype(jnp.bfloat16)
        v[:, pl.ds(2 * k, 1)] = yb[:, :128].reshape(16, 1, 16, 128)
        v[:, pl.ds(2 * k + 1, 1)] = yb[:, 128:].reshape(16, 1, 16, 128)
        return carry

    loads[1].wait()
    lax.fori_loop(0, 8, mid_step, 0)
    loads[2].wait()
    lax.fori_loop(8, 16, mid_step, 0)

    def code_step(o, carry):
        for c in range(3):
            codes[3 * o + c] = block_code(owner_map, o, c)
        return carry

    lax.fori_loop(0, 16, code_step, 0)
    xk[0] = jnp.full((16, 128), kind, F32)
    pl.semaphore_wait(barrier, 30)

    mate = (g + 1 - 2 * core, p)
    kind_copy = pltpu.make_async_remote_copy(
        xk.at[0], xk.at[1], xs_sem.at[16], xr_sem.at[16], device_id=mate, device_id_type=MESH
    )
    kind_copy.start()
    swaps = {}
    order = [(4, 0), (4, 1), (3, 1), (5, 0), (3, 0), (5, 1), (2, 1), (6, 0), (2, 0), (6, 1)]
    order += [(1, 1), (7, 0), (1, 0), (7, 1), (0, 0), (0, 1)]
    for d, h in order:
        z = lax.rem(zc + d, 8)
        swaps[d, h] = pltpu.make_async_remote_copy(
            v.at[2 * z + 1 - core, pl.ds(16 * h, 16)],
            xr.at[z, pl.ds(16 * h, 16)],
            xs_sem.at[2 * d + h],
            xr_sem.at[2 * d + h],
            device_id=mate,
            device_id_type=MESH,
        )
        swaps[d, h].start()
    kind_copy.wait_recv()
    other = xk[1][None]
    mine = kind
    swapped = set()

    def await_swap(d, h):
        if (d, h) not in swapped:
            swapped.add((d, h))
            swaps[d, h].wait_recv()

    def own_sum(z, at, k):
        me = v[2 * z + core, pl.ds(at, 4)].astype(F32)
        mate_part = xr[z, pl.ds(at, 4)].astype(F32)
        if k == 0:
            return me * (1.0 - mine) + mate_part * (1.0 - other)
        return me * mine + mate_part * other

    hops = {}

    def hop(k, n):
        for way in range(2):
            d = PLUS_D[n] if way == 0 else 8 - PLUS_D[n]
            h = PLUS_H[n] if way == 0 else 1 - PLUS_H[n]
            z = lax.rem(zc + d, 8)
            await_swap(d, h)
            if n >= 2:
                hops[k, way, n - 2].wait_recv()

            def add_step(a, carry):
                total = own_sum(z, 16 * h + 4 * a, k)
                if n >= 2:
                    total = total + rz[k, way, n - 2, pl.ds(4 * a, 4)].astype(F32)
                sb[k, way, n, pl.ds(4 * a, 4)] = total.astype(jnp.bfloat16)
                return carry

            lax.fori_loop(0, 4, add_step, 0)
            to = lax.rem(zc + (1 if way == 0 else 7), 8)
            hops[k, way, n] = pltpu.make_async_remote_copy(
                sb.at[k, way, n],
                rz.at[k, way, n],
                zs_sem.at[k, way, n],
                zr_sem.at[k, way, n],
                device_id=(2 * to + core, p),
                device_id_type=MESH,
            )
            hops[k, way, n].start()

    def tables():
        loads[3].wait()
        loads[4].wait()
        first = jnp.where(g == 0, 1, 0)
        for variant in range(3):
            var = variant * first
            for blk in range(4):

                def table_step(c, carry):
                    at = pl.ds(16 * c, 16)
                    me = masks[8 * var + 2 * blk]
                    mi = masks[8 * var + 2 * blk + 1]
                    val = ebuf[0, at].astype(F32) * me + ebuf[1, at].astype(F32) * mi
                    wbuf[variant, pl.ds(128 * blk + 16 * c, 16)] = val.astype(jnp.bfloat16)
                    return carry

                lax.fori_loop(0, 8, table_step, 0)

    def factors():
        lanes = lax.broadcasted_iota(jnp.int32, (8, 512), 1)
        k_long = jnp.where(lanes < 256, lanes, lanes - 512).astype(F32)
        r = lax.broadcasted_iota(jnp.int32, (128, 128), 0)
        i2, sign = (r >> 3) & 1, (r >> 4) & 1
        pair, grp = (r >> 5) & 1, (r >> 6) & 1
        pos = jnp.where(i2 == 0, 2 * g + pair, jnp.where((pair == 0) & (g == 0), 32, 64 - 2 * g - pair))
        base = jnp.where(grp == 0, -64 * sign, 64 - 192 * sign)
        k_mid = (pos + base).astype(F32)
        zi = 8 * p + (r & 7)
        k_z = jnp.where(zi < 64, zi, zi - 128).astype(F32)
        for k in range(2):
            mag = jnp.exp(diffusivity[k] * k_long * k_long * (-4.0 / 512**2))
            ph = velocity[k] * k_long * (-2.0 * math.pi / 256)
            flong[k, 0] = mag * jnp.cos(ph)
            flong[k, 1] = mag * jnp.sin(ph)
            d_mid = diffusivity[1 - k]
            v_mid = velocity[1 - k]
            mag = jnp.exp((d_mid * k_mid * k_mid + diffusivity[2] * k_z * k_z) * (-4.0 / 512**2)) * (1.0 / 4096)
            ph = (v_mid * k_mid + velocity[2] * k_z) * (-2.0 * math.pi / 256)
            frow[k, 0] = mag * jnp.cos(ph)
            frow[k, 1] = mag * jnp.sin(ph)

    def collect(k):
        for h in range(2):
            await_swap(0, h)
            a_way, b_way = (6, 5) if h == 0 else (5, 6)
            hops[k, 0, a_way].wait_recv()
            hops[k, 1, b_way].wait_recv()

            def last_step(a, carry):
                total = own_sum(zc, 16 * h + 4 * a, k)
                total = total + rz[k, 0, a_way, pl.ds(4 * a, 4)].astype(F32)
                total = total + rz[k, 1, b_way, pl.ds(4 * a, 4)].astype(F32)
                sf[k, pl.ds(256 * h + 64 * a, 64)] = total.reshape(64, 128)
                return carry

            lax.fori_loop(0, 4, last_step, 0)

    lane = lax.broadcasted_iota(jnp.int32, (64, 128), 1)
    low = lane < 64
    low32 = low[:32]
    lane32 = lane[:32] % 64
    swap = (lane32 >= 32) & (lane32 < 48) & (g == 0)

    def along_z(k):
        for grp in range(2):
            for pair in range(2):
                for e in range(4):
                    j = grp * 8 + pair * 4 + e
                    part = sf[k, pl.ds(j, 32, stride=16)].astype(jnp.bfloat16)
                    if pair == 0:
                        lhs0[k, grp, :, pl.ds(128 * e, 128)] = part
                    else:
                        lhs1[k, pl.ds(32 * grp, 32), pl.ds(128 * e, 128)] = part
        for t2 in range(4):
            cols = pl.ds(256 * t2, 256)
            wide_a = jnp.dot(lhs0[k, 0], wbuf[1, :, cols], preferred_element_type=F32)
            wide_b = jnp.dot(lhs0[k, 1], wbuf[2, :, cols], preferred_element_type=F32)
            wide_1 = jnp.dot(lhs1[k], wbuf[0, :, cols], preferred_element_type=F32)
            for t1 in range(2):
                t = 2 * t2 + t1
                part = slice(128 * t1, 128 * t1 + 128)
                ua, ub, u1 = wide_a[:, part], wide_b[:, part], wide_1[:, part]
                u1r = pltpu.roll(u1, 64, 1)
                for grp in range(2):
                    u0 = jnp.where(swap, ub, ua) if grp == 0 else jnp.where(swap, ua, ub)
                    u0r = pltpu.roll(u0, 64, 1)
                    at = slice(32 * grp, 32 * grp + 32)
                    chunk[k, 2 * t, grp] = jnp.where(low32, u0, u1r[at]).astype(jnp.bfloat16)
                    chunk[k, 2 * t + 1, grp] = jnp.where(low32, u0r, u1[at]).astype(jnp.bfloat16)

    outs = {}

    def send_lines(k):
        for s in (10, 11, 14, 9, 6, 15, 13, 7, 5, 8, 2, 12, 4, 3, 1):
            op = 4 * lax.rem(py + s // 4, 4) + lax.rem(px + s % 4, 4)
            outs[k, s] = pltpu.make_async_remote_copy(
                chunk.at[k, op],
                rows.at[k, p],
                ps_sem.at[k, s],
                pr_sem.at[k, s],
                device_id=(g, op),
                device_id_type=MESH,
            )
            outs[k, s].start()
        rows[k, pl.ds(p, 1)] = chunk[k, pl.ds(p, 1)]

    def along_long(k):
        for s in range(1, 16):
            outs[k, s].wait_recv()
        for grp in range(2):
            turned = rows[k, :, grp].reshape(512, 128).T
            for t in range(4):
                col_c = tlbuf[:, pl.ds(128 * t, 128)]
                col_s = tlbuf[:, pl.ds(512 + 128 * t, 128)]
                both = jnp.dot(turned, jnp.concatenate([col_c, col_s], axis=1), preferred_element_type=F32)
                c = both[:, :128].reshape(8, 2, 8, 128)
                sn = both[:, 128:].reshape(8, 2, 8, 128)
                re = c[:, 0] - sn[:, 1]
                im = c[:, 1] + sn[:, 0]
                rr = frow[k, 0, pl.ds(64 * grp, 64)].reshape(8, 8, 128)
                ri = frow[k, 1, pl.ds(64 * grp, 64)].reshape(8, 8, 128)
                lr = flong[k, 0, :, pl.ds(128 * t, 128)][None]
                li = flong[k, 1, :, pl.ds(128 * t, 128)][None]
                er = rr * lr - ri * li
                ei = rr * li + ri * lr
                out_re = re * er - im * ei
                out_im = re * ei + im * er
                full = jnp.stack([out_re, out_im], axis=1).reshape(2, 2, 2, 16, 128)
                spun = pltpu.roll(full.reshape(128, 128), 64, 1).reshape(2, 2, 2, 16, 128)
                for sign in range(2):
                    at = ((2 * k + grp) * 8 + t) * 2 + sign
                    ff[at] = full[:, sign].reshape(64, 128).astype(jnp.bfloat16)
                    ff[at + 8] = spun[:, sign].reshape(64, 128).astype(jnp.bfloat16)

    def piece(k, lb, gb, high):
        sign = gb >> 2
        grp = (gb & 1) ^ sign
        rot = (lb & 1) if high == 0 else 1 - (lb & 1)
        at = (((2 * k + grp) * 2 + rot) * 4 + (lb >> 1)) * 2 + sign
        return ff[at].astype(F32)

    finals = {}

    def send_pieces(k):
        for s in (8, 9, 7, 6, 10, 11, 5, 4, 12, 13, 3, 2, 14, 15, 1, 0):
            og = 2 * lax.rem(zc + s // 2, 8) + lax.rem(core + s % 2, 2)
            ca = codes[3 * og] >> 2
            cb = codes[3 * og + 1 + k] >> 2
            if k == 0:
                one, two = piece(0, ca >> 3, ca & 7, 0), piece(0, cb >> 3, cb & 7, 1)
            else:
                one, two = piece(1, ca & 7, ca >> 3, 0), piece(1, cb & 7, cb >> 3, 1)
            sb2[k, s] = jnp.where(low, one, two).astype(jnp.bfloat16)
            if s:
                copy = pltpu.make_async_remote_copy(
                    sb2.at[k, s],
                    landing.at[k, g],
                    gs_sem.at[k, s],
                    gr_sem.at[k, s],
                    device_id=(og, p),
                    device_id_type=MESH,
                )
            else:
                copy = pltpu.make_async_copy(sb2.at[k, 0], landing.at[k, g], gs_sem.at[k, 0])
            copy.start()
            finals[k, s] = copy

    for k, n in ((0, 0), (0, 1), (1, 0)):
        hop(k, n)
    tables()
    for k, n in ((0, 2), (0, 3), (1, 1)):
        hop(k, n)
    factors()
    for k, n in ((0, 4), (0, 5), (1, 2), (0, 6), (1, 3), (1, 4)):
        hop(k, n)
    collect(0)
    along_z(0)
    send_lines(0)
    hop(1, 5)
    hop(1, 6)
    collect(1)
    along_z(1)
    send_lines(1)
    loads[5].wait()
    for k in range(2):
        along_long(k)
        send_pieces(k)

    for copy in finals.values():
        copy.wait()
    for copy in outs.values():
        copy.wait_send()
    for copy in hops.values():
        copy.wait_send()
    for copy in swaps.values():
        copy.wait_send()
    kind_copy.wait_send()


def place_kernel(owner_map, landed, order, out, half, f0, d0, k0, sems):
    g = lax.axis_index("grid")
    copies = [pltpu.make_async_copy(landed.at[k], half.at[k], sems.at[k]) for k in range(2)]
    for copy in copies:
        copy.start()
    slot = [jnp.minimum(block_code(owner_map, g, c) & 3, 2) for c in range(3)]
    copies[0].wait()
    f0[...] = half[0].reshape(1024, 128).astype(F32)
    low32 = lax.broadcasted_iota(jnp.int32, (32, 128), 1) < 64
    low8 = low32[:8]
    for q in range(2):
        for z in range(8):
            rows = f0[pl.ds(8 * q + z, 64, stride=16)].astype(jnp.bfloat16)
            buf = z % 2
            d0[buf] = jnp.dot(rows.T, order[...], preferred_element_type=F32)
            for c in range(2):
                even = d0[buf, pl.ds(64 * c, 32, stride=2)]
                odd = d0[buf, pl.ds(64 * c + 1, 32, stride=2)]
                k0[c, q, pl.ds(z, 32, stride=8)] = jnp.where(low32, even, odd)
    copies[1].wait()
    for x2 in range(32):
        ge, ie = (x2, 0) if x2 < 16 else ((0, 1) if x2 == 16 else (32 - x2, 1))
        go, io = (x2, 2) if x2 < 16 else (31 - x2, 3)
        even = half[1, ge, pl.ds(16 * ie, 16)].astype(F32)
        odd = half[1, go, pl.ds(16 * io, 16)].astype(F32)
        for q in range(2):
            e, o = even[8 * q : 8 * q + 8], odd[8 * q : 8 * q + 8]
            first = jnp.where(low8, e, pltpu.roll(o, 64, 1))
            third = jnp.where(low8, pltpu.roll(e, 64, 1), o)
            at = pl.ds(8 * x2, 8)
            cols = pl.ds(128 * x2, 128)
            out[slot[0], q, :, cols] = first + k0[0, q, at]
            out[slot[1], q, :, cols] = k0[1, q, at]
            out[slot[2], q, :, cols] = third


def body(field, levels, coefficients, failed, owner_map, velocity, diffusivity):
    smem = pl.BlockSpec(memory_space=pltpu.SMEM)
    vmem = pl.BlockSpec(memory_space=pltpu.VMEM)
    anyspace = pl.BlockSpec(memory_space=pl.ANY)
    bf = jnp.bfloat16
    dma = pltpu.SemaphoreType.DMA
    landed = pl.pallas_call(
        transform_kernel,
        out_shape=jax.ShapeDtypeStruct((2, 16, 64, 128), bf),
        in_specs=[smem] * 6 + [anyspace] * 5,
        out_specs=anyspace,
        scratch_shapes=[
            pltpu.VMEM((32, 256, 128), bf),
            pltpu.VMEM((256, 256), bf),
            pltpu.VMEM((2, 128, 1024), bf),
            pltpu.VMEM((24, 1, 1024), F32),
            pltpu.VMEM((512, 1024), bf),
            pltpu.VMEM((3, 512, 1024), bf),
            pltpu.VMEM((16, 32, 16, 128), bf),
            pltpu.VMEM((8, 32, 16, 128), bf),
            pltpu.VMEM((2, 16, 128), F32),
            pltpu.VMEM((2, 2, 7, 16, 16, 128), bf),
            pltpu.VMEM((2, 2, 7, 16, 16, 128), bf),
            pltpu.VMEM((2, 512, 128), F32),
            pltpu.VMEM((2, 2, 32, 512), bf),
            pltpu.VMEM((2, 64, 512), bf),
            pltpu.VMEM((2, 16, 2, 32, 128), bf),
            pltpu.VMEM((2, 16, 2, 32, 128), bf),
            pltpu.VMEM((64, 64, 128), bf),
            pltpu.VMEM((2, 16, 64, 128), bf),
            pltpu.VMEM((2, 2, 8, 512), F32),
            pltpu.VMEM((2, 2, 128, 128), F32),
            pltpu.SMEM((48,), jnp.int32),
            dma((6,)), dma((17,)), dma((17,)), dma((2, 2, 7)), dma((2, 2, 7)),
            dma((2, 16)), dma((2, 16)), dma((2, 16)), dma((2, 16)),
        ],
        compiler_params=pltpu.CompilerParams(
            collective_id=0, has_side_effects=True, vmem_limit_bytes=56 * 2**20
        ),
        name="transform",
    )(
        levels, coefficients, failed, owner_map, velocity, diffusivity, field,
        jnp.asarray(mid_table()), jnp.asarray(z_bases()), jnp.asarray(z_masks()), jnp.asarray(long_table()),
    )
    return pl.pallas_call(
        place_kernel,
        out_shape=jax.ShapeDtypeStruct((3, 2, 8, 4096), F32),
        in_specs=[smem, anyspace, vmem],
        out_specs=vmem,
        scratch_shapes=[
            pltpu.VMEM((2, 16, 64, 128), bf),
            pltpu.VMEM((1024, 128), F32),
            pltpu.VMEM((2, 128, 128), F32),
            pltpu.VMEM((2, 2, 256, 128), F32),
            dma((2,)),
        ],
        compiler_params=pltpu.CompilerParams(vmem_limit_bytes=56 * 2**20),
        name="place",
    )(owner_map, landed, jnp.asarray(order_table()))


def solution(mesh):
    placed = (P("grid", "pencil", None, None), P("grid", None), P("grid"), P("grid"), P(), P(), P())
    return jax.shard_map(
        body, mesh=mesh, in_specs=placed, out_specs=P("grid", None, "pencil", None), check_vma=False
    )
```

```python
import functools
import math

import jax
import jax.numpy as jnp
import ml_dtypes
import numpy as np
from jax import lax
from jax.experimental import pallas as pl
from jax.experimental.pallas import tpu as pltpu
from jax.sharding import PartitionSpec as P

BF16 = ml_dtypes.bfloat16
F32 = jnp.float32
MESH = pl.DeviceIdType.MESH


def dft_table(length):
    positions = np.arange(length, dtype=np.int64)
    angles = (positions[:, None] * positions[None, :] % length) * (2.0 * math.pi / length)
    return np.cos(angles).astype(BF16).astype(np.float32), (-np.sin(angles)).astype(BF16).astype(np.float32)


def slot_positions(g):
    return [2 * g, 32 if g == 0 else 64 - 2 * g, 2 * g + 1, 63 - 2 * g]


@functools.cache
def mid_table():
    cos, sin = dft_table(256)
    rows = np.zeros((16, 2, 4, 2, 256), np.float32)
    for g in range(16):
        for grp in range(2):
            for i, n in enumerate(slot_positions(g)):
                rows[g, grp, i, 0] = cos[n + 64 * grp]
                rows[g, grp, i, 1] = sin[n + 64 * grp]
    rows[0, 0, 0, 1] = cos[128]
    return rows.reshape(256, 256).astype(BF16)


@functools.cache
def z_bases():
    cos, sin = dft_table(128)
    c = cos.reshape(16, 8, 128).transpose(2, 0, 1)
    s = sin.reshape(16, 8, 128).transpose(2, 0, 1)
    both = np.stack([np.stack([c, s], 2), np.stack([-s, c], 2)])
    full = np.broadcast_to(both[:, :, :, None], (2, 128, 16, 4, 2, 8))
    return full.reshape(2, 128, 1024).astype(BF16)


@functools.cache
def z_masks():
    out = np.zeros((3, 2, 2, 2, 16, 2, 2, 16), np.float32)

    def put(variant, i2, ab, sign, slot, which, scale):
        out[variant, i2, ab, which, :, sign, slot] = scale

    for variant in range(3):
        for i2 in range(2):
            if variant == 1 and i2 == 0:
                put(1, 0, 0, 0, 0, 0, 1.0)
                put(1, 0, 1, 1, 0, 0, 1.0)
                continue
            back = 1 - i2 if variant == 0 else i2
            put(variant, i2, 0, 0, i2, 0, 1.0)
            put(variant, i2, 1, 0, i2, 1, 1.0)
            put(variant, i2, 0, 1, back, 0, 1.0)
            put(variant, i2, 1, 1, back, 1, -1.0)
    return out.reshape(24, 1, 1024)


@functools.cache
def long_table():
    cos, sin = dft_table(512)
    return np.concatenate([cos, sin], axis=1).astype(BF16)


@functools.cache
def order_table():
    out = np.zeros((64, 128), np.float32)
    for g in range(16):
        for i, n in enumerate(slot_positions(g)):
            out[g * 4 + i, n] = 1.0
            out[g * 4 + i, n + 64] = 1.0
    return out.astype(BF16)


PLUS_D = (4, 3, 3, 2, 2, 1, 1)
PLUS_H = (0, 1, 0, 1, 0, 1, 0)
CLASSES = (
    tuple(8 * x + y for x in (0, 1, 6, 7) for y in (0, 1, 6, 7)),
    tuple(8 * x + y for x in (2, 3, 4, 5) for y in (0, 1, 6, 7)),
    tuple(8 * x + y for x in (0, 1, 6, 7) for y in (2, 3, 4, 5)),
)


def block_code(owner_map, owner, c):
    total = 0
    for b in CLASSES[c]:
        r = owner_map[b] - 3 * owner
        total = total + jnp.where((r >= 0) & (r < 3), 4 * b + r, 0)
    return total & 255


def transform_kernel(
    levels, coefficients, failed, owner_map, velocity, diffusivity, field, mid_tab, base_tab, mask_tab, long_tab,
    landing,
    fbuf, tbuf, ebuf, masks, tlbuf, wbuf, v, xr, xk, sb, rz, sf, lhs0, lhs1, chunk, rows, ff, sb2, flong, frow, codes,
    load_sem, xs_sem, xr_sem, zs_sem, zr_sem, ps_sem, pr_sem, gs_sem, gr_sem, row_sem,
):
    g = lax.axis_index("grid")
    p = lax.axis_index("pencil")
    zc, core = g // 2, g % 2
    py, px = p // 4, p % 4

    loads = [
        pltpu.make_async_copy(mid_tab, tbuf, load_sem.at[0]),
        pltpu.make_async_copy(field.at[0, pl.ds(0, 16)], fbuf.at[pl.ds(0, 16)], load_sem.at[1]),
        pltpu.make_async_copy(field.at[0, pl.ds(16, 16)], fbuf.at[pl.ds(16, 16)], load_sem.at[2]),
        pltpu.make_async_copy(base_tab, ebuf, load_sem.at[3]),
        pltpu.make_async_copy(mask_tab, masks, load_sem.at[4]),
        pltpu.make_async_copy(long_tab, tlbuf, load_sem.at[5]),
    ]
    for load in loads:
        load.start()

    barrier = pltpu.get_barrier_semaphore()
    for s in (2, 14, 1):
        og = 2 * lax.rem(zc + s // 2, 8) + lax.rem(core + s % 2, 2)
        pl.semaphore_signal(barrier, inc=1, device_id=(og, p), device_id_type=MESH)
    for s in (4, 8, 12, 1, 2, 3):
        op = 4 * lax.rem(py + s // 4, 4) + lax.rem(px + s % 4, 4)
        pl.semaphore_signal(barrier, inc=1, device_id=(g, op), device_id_type=MESH)

    kind = jnp.where(levels[0, 0] < levels[0, 1], 1.0, 0.0).astype(F32)
    weight = (coefficients[0] * (1 - failed[0])).astype(F32)
    loads[0].wait()

    def mid_step(k, carry):
        pair = jnp.concatenate([fbuf[2 * k], fbuf[2 * k + 1]], axis=1)
        y = jnp.dot(tbuf[...], pair, preferred_element_type=F32) * weight
        yb = y.astype(jnp.bfloat16)
        v[:, pl.ds(2 * k, 1)] = yb[:, :128].reshape(16, 1, 16, 128)
        v[:, pl.ds(2 * k + 1, 1)] = yb[:, 128:].reshape(16, 1, 16, 128)
        return carry

    loads[1].wait()
    lax.fori_loop(0, 8, mid_step, 0)
    loads[2].wait()
    lax.fori_loop(8, 16, mid_step, 0)

    xk[0] = jnp.full((16, 128), kind, F32)
    pl.semaphore_wait(barrier, 9)

    mate = (g + 1 - 2 * core, p)
    kind_copy = pltpu.make_async_remote_copy(
        xk.at[0], xk.at[1], xs_sem.at[16], xr_sem.at[16], device_id=mate, device_id_type=MESH
    )
    kind_copy.start()
    swaps = {}
    order = [(4, 0), (4, 1), (3, 1), (5, 0), (3, 0), (5, 1), (2, 1), (6, 0), (2, 0), (6, 1)]
    order += [(1, 1), (7, 0), (1, 0), (7, 1), (0, 0), (0, 1)]
    for d, h in order:
        z = lax.rem(zc + d, 8)
        swaps[d, h] = pltpu.make_async_remote_copy(
            v.at[2 * z + 1 - core, pl.ds(16 * h, 16)],
            xr.at[z, pl.ds(16 * h, 16)],
            xs_sem.at[2 * d + h],
            xr_sem.at[2 * d + h],
            device_id=mate,
            device_id_type=MESH,
        )
        swaps[d, h].start()
    kind_copy.wait_recv()
    other = xk[1][None]
    mine = kind
    swapped = set()

    def await_swap(d, h):
        if (d, h) not in swapped:
            swapped.add((d, h))
            swaps[d, h].wait_recv()

    def own_sum(z, at, k):
        me = v[2 * z + core, pl.ds(at, 4)].astype(F32)
        mate_part = xr[z, pl.ds(at, 4)].astype(F32)
        if k == 0:
            return me * (1.0 - mine) + mate_part * (1.0 - other)
        return me * mine + mate_part * other

    hops = {}

    def hop(k, n):
        for way in range(2):
            d = PLUS_D[n] if way == 0 else 8 - PLUS_D[n]
            h = PLUS_H[n] if way == 0 else 1 - PLUS_H[n]
            z = lax.rem(zc + d, 8)
            await_swap(d, h)
            if n >= 2:
                hops[k, way, n - 2].wait_recv()

            def add_step(a, carry):
                total = own_sum(z, 16 * h + 4 * a, k)
                if n >= 2:
                    total = total + rz[k, way, n - 2, pl.ds(4 * a, 4)].astype(F32)
                sb[k, way, n, pl.ds(4 * a, 4)] = total.astype(jnp.bfloat16)
                return carry

            lax.fori_loop(0, 4, add_step, 0)
            to = lax.rem(zc + (1 if way == 0 else 7), 8)
            hops[k, way, n] = pltpu.make_async_remote_copy(
                sb.at[k, way, n],
                rz.at[k, way, n],
                zs_sem.at[k, way, n],
                zr_sem.at[k, way, n],
                device_id=(2 * to + core, p),
                device_id_type=MESH,
            )
            hops[k, way, n].start()

    for s in range(1, 4):
        op = 4 * py + lax.rem(px + s, 4)
        pl.semaphore_signal(row_sem, inc=1, device_id=(g, op), device_id_type=MESH)

    def find_codes():
        def code_step(o, carry):
            for c in range(3):
                codes[3 * o + c] = block_code(owner_map, o, c)
            return carry

        lax.fori_loop(0, 16, code_step, 0)

    def tables():
        loads[3].wait()
        loads[4].wait()
        first = jnp.where(g == 0, 1, 0)
        for variant in range(3):
            var = variant * first
            for blk in range(4):

                def table_step(c, carry):
                    at = pl.ds(16 * c, 16)
                    me = masks[8 * var + 2 * blk]
                    mi = masks[8 * var + 2 * blk + 1]
                    val = ebuf[0, at].astype(F32) * me + ebuf[1, at].astype(F32) * mi
                    wbuf[variant, pl.ds(128 * blk + 16 * c, 16)] = val.astype(jnp.bfloat16)
                    return carry

                lax.fori_loop(0, 8, table_step, 0)

    def factors():
        lanes = lax.broadcasted_iota(jnp.int32, (8, 512), 1)
        k_long = jnp.where(lanes < 256, lanes, lanes - 512).astype(F32)
        r = lax.broadcasted_iota(jnp.int32, (128, 128), 0)
        i2, sign = (r >> 3) & 1, (r >> 4) & 1
        pair, grp = (r >> 5) & 1, (r >> 6) & 1
        pos = jnp.where(i2 == 0, 2 * g + pair, jnp.where((pair == 0) & (g == 0), 32, 64 - 2 * g - pair))
        base = jnp.where(grp == 0, -64 * sign, 64 - 192 * sign)
        k_mid = (pos + base).astype(F32)
        zi = 8 * p + (r & 7)
        k_z = jnp.where(zi < 64, zi, zi - 128).astype(F32)
        for k in range(2):
            mag = jnp.exp(diffusivity[k] * k_long * k_long * (-4.0 / 512**2))
            ph = velocity[k] * k_long * (-2.0 * math.pi / 256)
            flong[k, 0] = mag * jnp.cos(ph)
            flong[k, 1] = mag * jnp.sin(ph)
            d_mid = diffusivity[1 - k]
            v_mid = velocity[1 - k]
            mag = jnp.exp((d_mid * k_mid * k_mid + diffusivity[2] * k_z * k_z) * (-4.0 / 512**2)) * (1.0 / 4096)
            ph = (v_mid * k_mid + velocity[2] * k_z) * (-2.0 * math.pi / 256)
            frow[k, 0] = mag * jnp.cos(ph)
            frow[k, 1] = mag * jnp.sin(ph)

    def collect(k):
        for h in range(2):
            await_swap(0, h)
            a_way, b_way = (6, 5) if h == 0 else (5, 6)
            hops[k, 0, a_way].wait_recv()
            hops[k, 1, b_way].wait_recv()

            def last_step(a, carry):
                total = own_sum(zc, 16 * h + 4 * a, k)
                total = total + rz[k, 0, a_way, pl.ds(4 * a, 4)].astype(F32)
                total = total + rz[k, 1, b_way, pl.ds(4 * a, 4)].astype(F32)
                sf[k, pl.ds(256 * h + 64 * a, 64)] = total.reshape(64, 128)
                return carry

            lax.fori_loop(0, 4, last_step, 0)

    lane = lax.broadcasted_iota(jnp.int32, (64, 128), 1)
    low = lane < 64
    low32 = low[:32]
    lane32 = lane[:32] % 64
    swap = (lane32 >= 32) & (lane32 < 48) & (g == 0)

    def along_z(k):
        for grp in range(2):
            for pair in range(2):
                for e in range(4):
                    j = grp * 8 + pair * 4 + e
                    part = sf[k, pl.ds(j, 32, stride=16)].astype(jnp.bfloat16)
                    if pair == 0:
                        lhs0[k, grp, :, pl.ds(128 * e, 128)] = part
                    else:
                        lhs1[k, pl.ds(32 * grp, 32), pl.ds(128 * e, 128)] = part
        for t2 in range(4):
            cols = pl.ds(256 * t2, 256)
            wide_a = jnp.dot(lhs0[k, 0], wbuf[1, :, cols], preferred_element_type=F32)
            wide_b = jnp.dot(lhs0[k, 1], wbuf[2, :, cols], preferred_element_type=F32)
            wide_1 = jnp.dot(lhs1[k], wbuf[0, :, cols], preferred_element_type=F32)
            for t1 in range(2):
                t = 2 * t2 + t1
                part = slice(128 * t1, 128 * t1 + 128)
                ua, ub, u1 = wide_a[:, part], wide_b[:, part], wide_1[:, part]
                u1r = pltpu.roll(u1, 64, 1)
                for grp in range(2):
                    u0 = jnp.where(swap, ub, ua) if grp == 0 else jnp.where(swap, ua, ub)
                    u0r = pltpu.roll(u0, 64, 1)
                    at = slice(32 * grp, 32 * grp + 32)
                    chunk[k, 2 * t, grp] = jnp.where(low32, u0, u1r[at]).astype(jnp.bfloat16)
                    chunk[k, 2 * t + 1, grp] = jnp.where(low32, u0r, u1[at]).astype(jnp.bfloat16)

    outs = {}

    def send_lines(k):
        for s in (10, 11, 14, 9, 6, 15, 13, 7, 5, 8, 2, 12, 4, 3, 1):
            op = 4 * lax.rem(py + s // 4, 4) + lax.rem(px + s % 4, 4)
            outs[k, s] = pltpu.make_async_remote_copy(
                chunk.at[k, op],
                rows.at[k, p],
                ps_sem.at[k, s],
                pr_sem.at[k, s],
                device_id=(g, op),
                device_id_type=MESH,
            )
            outs[k, s].start()
        rows[k, pl.ds(p, 1)] = chunk[k, pl.ds(p, 1)]

    def along_long(k):
        for s in range(1, 16):
            outs[k, s].wait_recv()
        for grp in range(2):
            turned = rows[k, :, grp].reshape(512, 128).T
            for t in range(4):
                col_c = tlbuf[:, pl.ds(128 * t, 128)]
                col_s = tlbuf[:, pl.ds(512 + 128 * t, 128)]
                both = jnp.dot(turned, jnp.concatenate([col_c, col_s], axis=1), preferred_element_type=F32)
                c = both[:, :128].reshape(8, 2, 8, 128)
                sn = both[:, 128:].reshape(8, 2, 8, 128)
                re = c[:, 0] - sn[:, 1]
                im = c[:, 1] + sn[:, 0]
                rr = frow[k, 0, pl.ds(64 * grp, 64)].reshape(8, 8, 128)
                ri = frow[k, 1, pl.ds(64 * grp, 64)].reshape(8, 8, 128)
                lr = flong[k, 0, :, pl.ds(128 * t, 128)][None]
                li = flong[k, 1, :, pl.ds(128 * t, 128)][None]
                er = rr * lr - ri * li
                ei = rr * li + ri * lr
                out_re = re * er - im * ei
                out_im = re * ei + im * er
                full = jnp.stack([out_re, out_im], axis=1).reshape(2, 2, 2, 16, 128)
                spun = pltpu.roll(full.reshape(128, 128), 64, 1).reshape(2, 2, 2, 16, 128)
                for sign in range(2):
                    at = ((2 * k + grp) * 8 + t) * 2 + sign
                    ff[at] = full[:, sign].reshape(64, 128).astype(jnp.bfloat16)
                    ff[at + 8] = spun[:, sign].reshape(64, 128).astype(jnp.bfloat16)

    def piece(k, lb, gb, high):
        sign = gb >> 2
        grp = (gb & 1) ^ sign
        rot = (lb & 1) if high == 0 else 1 - (lb & 1)
        at = (((2 * k + grp) * 2 + rot) * 4 + (lb >> 1)) * 2 + sign
        return ff[at].astype(F32)

    finals = {}

    def send_pieces(k):
        for s in (8, 9, 7, 6, 10, 11, 5, 4, 12, 13, 3, 2, 14, 15, 1, 0):
            og = 2 * lax.rem(zc + s // 2, 8) + lax.rem(core + s % 2, 2)
            ca = codes[3 * og] >> 2
            cb = codes[3 * og + 1 + k] >> 2
            if k == 0:
                one, two = piece(0, ca >> 3, ca & 7, 0), piece(0, cb >> 3, cb & 7, 1)
            else:
                one, two = piece(1, ca & 7, ca >> 3, 0), piece(1, cb & 7, cb >> 3, 1)
            sb2[k, s] = jnp.where(low, one, two).astype(jnp.bfloat16)
            if s:
                copy = pltpu.make_async_remote_copy(
                    sb2.at[k, s],
                    landing.at[k, g],
                    gs_sem.at[k, s],
                    gr_sem.at[k, s],
                    device_id=(og, p),
                    device_id_type=MESH,
                )
            else:
                copy = pltpu.make_async_copy(sb2.at[k, 0], landing.at[k, g], gs_sem.at[k, 0])
            copy.start()
            finals[k, s] = copy

    for k, n in ((0, 0), (0, 1), (1, 0)):
        hop(k, n)
    tables()
    for k, n in ((0, 2), (0, 3), (1, 1)):
        hop(k, n)
    find_codes()
    for k, n in ((0, 4), (0, 5), (1, 2)):
        hop(k, n)
    factors()
    for k, n in ((0, 6), (1, 3), (1, 4)):
        hop(k, n)
    collect(0)
    along_z(0)
    pl.semaphore_wait(row_sem, 3)
    send_lines(0)
    hop(1, 5)
    hop(1, 6)
    collect(1)
    along_z(1)
    send_lines(1)
    loads[5].wait()
    for k in range(2):
        along_long(k)
        send_pieces(k)

    for copy in finals.values():
        copy.wait()
    for copy in outs.values():
        copy.wait_send()
    for copy in hops.values():
        copy.wait_send()
    for copy in swaps.values():
        copy.wait_send()
    kind_copy.wait_send()


def place_kernel(owner_map, landed, order, out, half, f0, d0, k0, staged, sems):
    g = lax.axis_index("grid")
    copies = [pltpu.make_async_copy(landed.at[k], half.at[k], sems.at[k]) for k in range(2)]
    for copy in copies:
        copy.start()
    slot = [jnp.minimum(block_code(owner_map, g, c) & 3, 2) for c in range(3)]
    puts = [pltpu.make_async_copy(staged.at[c], out.at[slot[c]], sems.at[2 + c]) for c in range(3)]
    copies[0].wait()
    f0[...] = half[0].reshape(1024, 128).astype(F32)
    low32 = lax.broadcasted_iota(jnp.int32, (32, 128), 1) < 64
    low8 = low32[:8]
    for q in range(2):
        for z in range(8):
            rows = f0[pl.ds(8 * q + z, 64, stride=16)].astype(jnp.bfloat16)
            buf = 8 * q + z
            d0[buf] = jnp.dot(rows.T, order[...], preferred_element_type=F32)
            for c in range(2):
                even = d0[buf, pl.ds(64 * c, 32, stride=2)]
                odd = d0[buf, pl.ds(64 * c + 1, 32, stride=2)]
                k0[c, q, pl.ds(z, 32, stride=8)] = jnp.where(low32, even, odd)
        for x2 in range(32):
            staged[1, q, :, pl.ds(128 * x2, 128)] = k0[1, q, pl.ds(8 * x2, 8)]
    puts[1].start()
    copies[1].wait()
    for x2 in range(32):
        ge, ie = (x2, 0) if x2 < 16 else ((0, 1) if x2 == 16 else (32 - x2, 1))
        go, io = (x2, 2) if x2 < 16 else (31 - x2, 3)
        even = half[1, ge, pl.ds(16 * ie, 16)].astype(F32)
        odd = half[1, go, pl.ds(16 * io, 16)].astype(F32)
        for q in range(2):
            e, o = even[8 * q : 8 * q + 8], odd[8 * q : 8 * q + 8]
            first = jnp.where(low8, e, pltpu.roll(o, 64, 1))
            third = jnp.where(low8, pltpu.roll(e, 64, 1), o)
            cols = pl.ds(128 * x2, 128)
            staged[0, q, :, cols] = first + k0[0, q, pl.ds(8 * x2, 8)]
            staged[2, q, :, cols] = third
    puts[0].start()
    puts[2].start()
    for put in puts:
        put.wait()


def body(field, levels, coefficients, failed, owner_map, velocity, diffusivity):
    smem = pl.BlockSpec(memory_space=pltpu.SMEM)
    vmem = pl.BlockSpec(memory_space=pltpu.VMEM)
    anyspace = pl.BlockSpec(memory_space=pl.ANY)
    bf = jnp.bfloat16
    dma = pltpu.SemaphoreType.DMA
    landed = pl.pallas_call(
        transform_kernel,
        out_shape=jax.ShapeDtypeStruct((2, 16, 64, 128), bf),
        in_specs=[smem] * 6 + [anyspace] * 5,
        out_specs=anyspace,
        scratch_shapes=[
            pltpu.VMEM((32, 256, 128), bf),
            pltpu.VMEM((256, 256), bf),
            pltpu.VMEM((2, 128, 1024), bf),
            pltpu.VMEM((24, 1, 1024), F32),
            pltpu.VMEM((512, 1024), bf),
            pltpu.VMEM((3, 512, 1024), bf),
            pltpu.VMEM((16, 32, 16, 128), bf),
            pltpu.VMEM((8, 32, 16, 128), bf),
            pltpu.VMEM((2, 16, 128), F32),
            pltpu.VMEM((2, 2, 7, 16, 16, 128), bf),
            pltpu.VMEM((2, 2, 7, 16, 16, 128), bf),
            pltpu.VMEM((2, 512, 128), F32),
            pltpu.VMEM((2, 2, 32, 512), bf),
            pltpu.VMEM((2, 64, 512), bf),
            pltpu.VMEM((2, 16, 2, 32, 128), bf),
            pltpu.VMEM((2, 16, 2, 32, 128), bf),
            pltpu.VMEM((64, 64, 128), bf),
            pltpu.VMEM((2, 16, 64, 128), bf),
            pltpu.VMEM((2, 2, 8, 512), F32),
            pltpu.VMEM((2, 2, 128, 128), F32),
            pltpu.SMEM((48,), jnp.int32),
            dma((6,)), dma((17,)), dma((17,)), dma((2, 2, 7)), dma((2, 2, 7)),
            dma((2, 16)), dma((2, 16)), dma((2, 16)), dma((2, 16)),
            pltpu.SemaphoreType.REGULAR,
        ],
        compiler_params=pltpu.CompilerParams(
            collective_id=0, has_side_effects=True, vmem_limit_bytes=56 * 2**20
        ),
        name="transform",
    )(
        levels, coefficients, failed, owner_map, velocity, diffusivity, field,
        jnp.asarray(mid_table()), jnp.asarray(z_bases()), jnp.asarray(z_masks()), jnp.asarray(long_table()),
    )
    return pl.pallas_call(
        place_kernel,
        out_shape=jax.ShapeDtypeStruct((3, 2, 8, 4096), F32),
        in_specs=[smem, anyspace, vmem],
        out_specs=anyspace,
        scratch_shapes=[
            pltpu.VMEM((2, 16, 64, 128), bf),
            pltpu.VMEM((1024, 128), F32),
            pltpu.VMEM((16, 128, 128), F32),
            pltpu.VMEM((2, 2, 256, 128), F32),
            pltpu.VMEM((3, 2, 8, 4096), F32),
            dma((5,)),
        ],
        compiler_params=pltpu.CompilerParams(vmem_limit_bytes=56 * 2**20),
        name="place",
    )(owner_map, landed, jnp.asarray(order_table()))


def solution(mesh):
    placed = (P("grid", "pencil", None, None), P("grid", None), P("grid"), P("grid"), P(), P(), P())
    return jax.shard_map(
        body, mesh=mesh, in_specs=placed, out_specs=P("grid", None, "pencil", None), check_vma=False
    )
```

```python
import functools
import math

import jax
import jax.numpy as jnp
import ml_dtypes
import numpy as np
from jax import lax
from jax.experimental import pallas as pl
from jax.experimental.pallas import tpu as pltpu
from jax.sharding import PartitionSpec as P

BF16 = ml_dtypes.bfloat16
F32 = jnp.float32
MESH = pl.DeviceIdType.MESH


def dft_table(length):
    positions = np.arange(length, dtype=np.int64)
    angles = (positions[:, None] * positions[None, :] % length) * (2.0 * math.pi / length)
    return np.cos(angles).astype(BF16).astype(np.float32), (-np.sin(angles)).astype(BF16).astype(np.float32)


def slot_positions(g):
    return [2 * g, 32 if g == 0 else 64 - 2 * g, 2 * g + 1, 63 - 2 * g]


@functools.cache
def mid_table():
    cos, sin = dft_table(256)
    rows = np.zeros((16, 2, 4, 2, 256), np.float32)
    for g in range(16):
        for grp in range(2):
            for i, n in enumerate(slot_positions(g)):
                rows[g, grp, i, 0] = cos[n + 64 * grp]
                rows[g, grp, i, 1] = sin[n + 64 * grp]
    rows[0, 0, 0, 1] = cos[128]
    return rows.reshape(256, 256).astype(BF16)


@functools.cache
def z_bases():
    cos, sin = dft_table(128)
    c = cos.reshape(16, 8, 128).transpose(2, 0, 1)
    s = sin.reshape(16, 8, 128).transpose(2, 0, 1)
    both = np.stack([np.stack([c, s], 2), np.stack([-s, c], 2)])
    full = np.broadcast_to(both[:, :, :, None], (2, 128, 16, 4, 2, 8))
    return full.reshape(2, 128, 1024).astype(BF16)


@functools.cache
def z_masks():
    out = np.zeros((3, 2, 2, 2, 16, 2, 2, 16), np.float32)

    def put(variant, i2, ab, sign, slot, which, scale):
        out[variant, i2, ab, which, :, sign, slot] = scale

    for variant in range(3):
        for i2 in range(2):
            if variant == 1 and i2 == 0:
                put(1, 0, 0, 0, 0, 0, 1.0)
                put(1, 0, 1, 1, 0, 0, 1.0)
                continue
            back = 1 - i2 if variant == 0 else i2
            put(variant, i2, 0, 0, i2, 0, 1.0)
            put(variant, i2, 1, 0, i2, 1, 1.0)
            put(variant, i2, 0, 1, back, 0, 1.0)
            put(variant, i2, 1, 1, back, 1, -1.0)
    return out.reshape(24, 1, 1024)


@functools.cache
def long_table():
    cos, sin = dft_table(512)
    return np.concatenate([cos, sin], axis=1).astype(BF16)


@functools.cache
def order_table():
    out = np.zeros((64, 128), np.float32)
    for g in range(16):
        for i, n in enumerate(slot_positions(g)):
            out[g * 4 + i, n] = 1.0
            out[g * 4 + i, n + 64] = 1.0
    return out.astype(BF16)


PLUS_D = (4, 3, 3, 2, 2, 1, 1)
PLUS_H = (0, 1, 0, 1, 0, 1, 0)
CLASSES = (
    tuple(8 * x + y for x in (0, 1, 6, 7) for y in (0, 1, 6, 7)),
    tuple(8 * x + y for x in (2, 3, 4, 5) for y in (0, 1, 6, 7)),
    tuple(8 * x + y for x in (0, 1, 6, 7) for y in (2, 3, 4, 5)),
)


def block_code(owner_map, owner, c):
    total = 0
    for b in CLASSES[c]:
        r = owner_map[b] - 3 * owner
        total = total + jnp.where((r >= 0) & (r < 3), 4 * b + r, 0)
    return total & 255


def transform_kernel(
    levels, coefficients, failed, owner_map, velocity, diffusivity, field, mid_tab, base_tab, mask_tab, long_tab,
    landing,
    fbuf, tbuf, ebuf, masks, tlbuf, wbuf, v, xr, xk, sb, rz, sf, lhs0, lhs1, chunk, rows, ff, sb2, flong, frow, codes,
    load_sem, xs_sem, xr_sem, zs_sem, zr_sem, ps_sem, pr_sem, gs_sem, gr_sem, row_sem,
):
    g = lax.axis_index("grid")
    p = lax.axis_index("pencil")
    zc, core = g // 2, g % 2
    py, px = p // 4, p % 4

    loads = [
        pltpu.make_async_copy(mid_tab, tbuf, load_sem.at[0]),
        pltpu.make_async_copy(field.at[0, pl.ds(0, 16)], fbuf.at[pl.ds(0, 16)], load_sem.at[1]),
        pltpu.make_async_copy(field.at[0, pl.ds(16, 16)], fbuf.at[pl.ds(16, 16)], load_sem.at[2]),
        pltpu.make_async_copy(base_tab, ebuf, load_sem.at[3]),
        pltpu.make_async_copy(mask_tab, masks, load_sem.at[4]),
        pltpu.make_async_copy(long_tab, tlbuf, load_sem.at[5]),
    ]
    for load in loads:
        load.start()

    barrier = pltpu.get_barrier_semaphore()
    for s in (2, 14, 1):
        og = 2 * lax.rem(zc + s // 2, 8) + lax.rem(core + s % 2, 2)
        pl.semaphore_signal(barrier, inc=1, device_id=(og, p), device_id_type=MESH)
    for s in (4, 8, 12, 1, 2, 3):
        op = 4 * lax.rem(py + s // 4, 4) + lax.rem(px + s % 4, 4)
        pl.semaphore_signal(barrier, inc=1, device_id=(g, op), device_id_type=MESH)

    kind = jnp.where(levels[0, 0] < levels[0, 1], 1.0, 0.0).astype(F32)
    weight = (coefficients[0] * (1 - failed[0])).astype(F32)
    loads[0].wait()

    def mid_step(k, carry):
        pair = jnp.concatenate([fbuf[2 * k], fbuf[2 * k + 1]], axis=1)
        y = jnp.dot(tbuf[...], pair, preferred_element_type=F32) * weight
        yb = y.astype(jnp.bfloat16)
        v[:, pl.ds(2 * k, 1)] = yb[:, :128].reshape(16, 1, 16, 128)
        v[:, pl.ds(2 * k + 1, 1)] = yb[:, 128:].reshape(16, 1, 16, 128)
        return carry

    loads[1].wait()
    lax.fori_loop(0, 8, mid_step, 0, unroll=4)
    loads[2].wait()
    lax.fori_loop(8, 16, mid_step, 0, unroll=4)

    xk[0] = jnp.full((16, 128), kind, F32)
    pl.semaphore_wait(barrier, 9)

    mate = (g + 1 - 2 * core, p)
    kind_copy = pltpu.make_async_remote_copy(
        xk.at[0], xk.at[1], xs_sem.at[16], xr_sem.at[16], device_id=mate, device_id_type=MESH
    )
    kind_copy.start()
    swaps = {}
    order = [(4, 0), (4, 1), (3, 1), (5, 0), (3, 0), (5, 1), (2, 1), (6, 0), (2, 0), (6, 1)]
    order += [(1, 1), (7, 0), (1, 0), (7, 1), (0, 0), (0, 1)]
    for d, h in order:
        z = lax.rem(zc + d, 8)
        swaps[d, h] = pltpu.make_async_remote_copy(
            v.at[2 * z + 1 - core, pl.ds(16 * h, 16)],
            xr.at[z, pl.ds(16 * h, 16)],
            xs_sem.at[2 * d + h],
            xr_sem.at[2 * d + h],
            device_id=mate,
            device_id_type=MESH,
        )
        swaps[d, h].start()
    kind_copy.wait_recv()
    other = xk[1][None]
    mine = kind
    swapped = set()

    def await_swap(d, h):
        if (d, h) not in swapped:
            swapped.add((d, h))
            swaps[d, h].wait_recv()

    def own_sum(z, at, k):
        me = v[2 * z + core, pl.ds(at, 4)].astype(F32)
        mate_part = xr[z, pl.ds(at, 4)].astype(F32)
        if k == 0:
            return me * (1.0 - mine) + mate_part * (1.0 - other)
        return me * mine + mate_part * other

    hops = {}

    def hop(k, n):
        for way in range(2):
            d = PLUS_D[n] if way == 0 else 8 - PLUS_D[n]
            h = PLUS_H[n] if way == 0 else 1 - PLUS_H[n]
            z = lax.rem(zc + d, 8)
            await_swap(d, h)
            if n >= 2:
                hops[k, way, n - 2].wait_recv()

            def add_step(a, carry):
                total = own_sum(z, 16 * h + 4 * a, k)
                if n >= 2:
                    total = total + rz[k, way, n - 2, pl.ds(4 * a, 4)].astype(F32)
                sb[k, way, n, pl.ds(4 * a, 4)] = total.astype(jnp.bfloat16)
                return carry

            lax.fori_loop(0, 4, add_step, 0)
            to = lax.rem(zc + (1 if way == 0 else 7), 8)
            hops[k, way, n] = pltpu.make_async_remote_copy(
                sb.at[k, way, n],
                rz.at[k, way, n],
                zs_sem.at[k, way, n],
                zr_sem.at[k, way, n],
                device_id=(2 * to + core, p),
                device_id_type=MESH,
            )
            hops[k, way, n].start()

    for s in range(1, 4):
        op = 4 * py + lax.rem(px + s, 4)
        pl.semaphore_signal(row_sem, inc=1, device_id=(g, op), device_id_type=MESH)

    def find_codes():
        def code_step(o, carry):
            for c in range(3):
                codes[3 * o + c] = block_code(owner_map, o, c)
            return carry

        lax.fori_loop(0, 16, code_step, 0)

    def tables():
        loads[3].wait()
        loads[4].wait()
        first = jnp.where(g == 0, 1, 0)
        for variant in range(3):
            var = variant * first
            for blk in range(4):

                def table_step(c, carry):
                    at = pl.ds(16 * c, 16)
                    me = masks[8 * var + 2 * blk]
                    mi = masks[8 * var + 2 * blk + 1]
                    val = ebuf[0, at].astype(F32) * me + ebuf[1, at].astype(F32) * mi
                    wbuf[variant, pl.ds(128 * blk + 16 * c, 16)] = val.astype(jnp.bfloat16)
                    return carry

                lax.fori_loop(0, 8, table_step, 0)

    def factors():
        lanes = lax.broadcasted_iota(jnp.int32, (8, 512), 1)
        k_long = jnp.where(lanes < 256, lanes, lanes - 512).astype(F32)
        r = lax.broadcasted_iota(jnp.int32, (128, 128), 0)
        i2, sign = (r >> 3) & 1, (r >> 4) & 1
        pair, grp = (r >> 5) & 1, (r >> 6) & 1
        pos = jnp.where(i2 == 0, 2 * g + pair, jnp.where((pair == 0) & (g == 0), 32, 64 - 2 * g - pair))
        base = jnp.where(grp == 0, -64 * sign, 64 - 192 * sign)
        k_mid = (pos + base).astype(F32)
        zi = 8 * p + (r & 7)
        k_z = jnp.where(zi < 64, zi, zi - 128).astype(F32)
        for k in range(2):
            mag = jnp.exp(diffusivity[k] * k_long * k_long * (-4.0 / 512**2))
            ph = velocity[k] * k_long * (-2.0 * math.pi / 256)
            flong[k, 0] = mag * jnp.cos(ph)
            flong[k, 1] = mag * jnp.sin(ph)
            d_mid = diffusivity[1 - k]
            v_mid = velocity[1 - k]
            mag = jnp.exp((d_mid * k_mid * k_mid + diffusivity[2] * k_z * k_z) * (-4.0 / 512**2)) * (1.0 / 4096)
            ph = (v_mid * k_mid + velocity[2] * k_z) * (-2.0 * math.pi / 256)
            frow[k, 0] = mag * jnp.cos(ph)
            frow[k, 1] = mag * jnp.sin(ph)

    def collect(k):
        for h in range(2):
            await_swap(0, h)
            a_way, b_way = (6, 5) if h == 0 else (5, 6)
            hops[k, 0, a_way].wait_recv()
            hops[k, 1, b_way].wait_recv()

            def last_step(a, carry):
                total = own_sum(zc, 16 * h + 4 * a, k)
                total = total + rz[k, 0, a_way, pl.ds(4 * a, 4)].astype(F32)
                total = total + rz[k, 1, b_way, pl.ds(4 * a, 4)].astype(F32)
                sf[k, pl.ds(256 * h + 64 * a, 64)] = total.reshape(64, 128)
                return carry

            lax.fori_loop(0, 4, last_step, 0)

    lane = lax.broadcasted_iota(jnp.int32, (64, 128), 1)
    low = lane < 64
    low32 = low[:32]
    lane32 = lane[:32] % 64
    swap = (lane32 >= 32) & (lane32 < 48) & (g == 0)

    def along_z(k):
        for grp in range(2):
            for pair in range(2):
                for e in range(4):
                    j = grp * 8 + pair * 4 + e
                    part = sf[k, pl.ds(j, 32, stride=16)].astype(jnp.bfloat16)
                    if pair == 0:
                        lhs0[k, grp, :, pl.ds(128 * e, 128)] = part
                    else:
                        lhs1[k, pl.ds(32 * grp, 32), pl.ds(128 * e, 128)] = part
        for t2 in range(4):
            cols = pl.ds(256 * t2, 256)
            wide_a = jnp.dot(lhs0[k, 0], wbuf[1, :, cols], preferred_element_type=F32)
            wide_b = jnp.dot(lhs0[k, 1], wbuf[2, :, cols], preferred_element_type=F32)
            wide_1 = jnp.dot(lhs1[k], wbuf[0, :, cols], preferred_element_type=F32)
            for t1 in range(2):
                t = 2 * t2 + t1
                part = slice(128 * t1, 128 * t1 + 128)
                ua, ub, u1 = wide_a[:, part], wide_b[:, part], wide_1[:, part]
                u1r = pltpu.roll(u1, 64, 1)
                for grp in range(2):
                    u0 = jnp.where(swap, ub, ua) if grp == 0 else jnp.where(swap, ua, ub)
                    u0r = pltpu.roll(u0, 64, 1)
                    at = slice(32 * grp, 32 * grp + 32)
                    chunk[k, 2 * t, grp] = jnp.where(low32, u0, u1r[at]).astype(jnp.bfloat16)
                    chunk[k, 2 * t + 1, grp] = jnp.where(low32, u0r, u1[at]).astype(jnp.bfloat16)

    outs = {}

    def send_lines(k):
        for s in (10, 11, 14, 9, 6, 15, 13, 7, 5, 8, 2, 12, 4, 3, 1):
            op = 4 * lax.rem(py + s // 4, 4) + lax.rem(px + s % 4, 4)
            outs[k, s] = pltpu.make_async_remote_copy(
                chunk.at[k, op],
                rows.at[k, p],
                ps_sem.at[k, s],
                pr_sem.at[k, s],
                device_id=(g, op),
                device_id_type=MESH,
            )
            outs[k, s].start()
        rows[k, pl.ds(p, 1)] = chunk[k, pl.ds(p, 1)]

    def along_long(k):
        for s in range(1, 16):
            outs[k, s].wait_recv()
        for grp in range(2):
            turned = rows[k, :, grp].reshape(512, 128).T
            for t in range(4):
                col_c = tlbuf[:, pl.ds(128 * t, 128)]
                col_s = tlbuf[:, pl.ds(512 + 128 * t, 128)]
                both = jnp.dot(turned, jnp.concatenate([col_c, col_s], axis=1), preferred_element_type=F32)
                c = both[:, :128].reshape(8, 2, 8, 128)
                sn = both[:, 128:].reshape(8, 2, 8, 128)
                re = c[:, 0] - sn[:, 1]
                im = c[:, 1] + sn[:, 0]
                rr = frow[k, 0, pl.ds(64 * grp, 64)].reshape(8, 8, 128)
                ri = frow[k, 1, pl.ds(64 * grp, 64)].reshape(8, 8, 128)
                lr = flong[k, 0, :, pl.ds(128 * t, 128)][None]
                li = flong[k, 1, :, pl.ds(128 * t, 128)][None]
                er = rr * lr - ri * li
                ei = rr * li + ri * lr
                out_re = re * er - im * ei
                out_im = re * ei + im * er
                full = jnp.stack([out_re, out_im], axis=1).reshape(2, 2, 2, 16, 128)
                spun = pltpu.roll(full.reshape(128, 128), 64, 1).reshape(2, 2, 2, 16, 128)
                for sign in range(2):
                    at = ((2 * k + grp) * 8 + t) * 2 + sign
                    ff[at] = full[:, sign].reshape(64, 128).astype(jnp.bfloat16)
                    ff[at + 8] = spun[:, sign].reshape(64, 128).astype(jnp.bfloat16)

    def piece(k, lb, gb, high):
        sign = gb >> 2
        grp = (gb & 1) ^ sign
        rot = (lb & 1) if high == 0 else 1 - (lb & 1)
        at = (((2 * k + grp) * 2 + rot) * 4 + (lb >> 1)) * 2 + sign
        return ff[at].astype(F32)

    finals = {}

    def send_pieces(k):
        for s in (8, 9, 7, 6, 10, 11, 5, 4, 12, 13, 3, 2, 14, 15, 1, 0):
            og = 2 * lax.rem(zc + s // 2, 8) + lax.rem(core + s % 2, 2)
            ca = codes[3 * og] >> 2
            cb = codes[3 * og + 1 + k] >> 2
            if k == 0:
                one, two = piece(0, ca >> 3, ca & 7, 0), piece(0, cb >> 3, cb & 7, 1)
            else:
                one, two = piece(1, ca & 7, ca >> 3, 0), piece(1, cb & 7, cb >> 3, 1)
            sb2[k, s] = jnp.where(low, one, two).astype(jnp.bfloat16)
            if s:
                copy = pltpu.make_async_remote_copy(
                    sb2.at[k, s],
                    landing.at[k, g],
                    gs_sem.at[k, s],
                    gr_sem.at[k, s],
                    device_id=(og, p),
                    device_id_type=MESH,
                )
            else:
                copy = pltpu.make_async_copy(sb2.at[k, 0], landing.at[k, g], gs_sem.at[k, 0])
            copy.start()
            finals[k, s] = copy

    for k, n in ((0, 0), (0, 1), (1, 0)):
        hop(k, n)
    tables()
    for k, n in ((0, 2), (0, 3), (1, 1)):
        hop(k, n)
    find_codes()
    for k, n in ((0, 4), (0, 5), (1, 2)):
        hop(k, n)
    factors()
    for k, n in ((0, 6), (1, 3), (1, 4)):
        hop(k, n)
    collect(0)
    along_z(0)
    pl.semaphore_wait(row_sem, 3)
    send_lines(0)
    hop(1, 5)
    hop(1, 6)
    collect(1)
    along_z(1)
    send_lines(1)
    loads[5].wait()
    for k in range(2):
        along_long(k)
        send_pieces(k)

    for copy in finals.values():
        copy.wait()
    for copy in outs.values():
        copy.wait_send()
    for copy in hops.values():
        copy.wait_send()
    for copy in swaps.values():
        copy.wait_send()
    kind_copy.wait_send()


def place_kernel(owner_map, landed, order, out, half, f0, d0, k0, staged, sems):
    g = lax.axis_index("grid")
    copies = [pltpu.make_async_copy(landed.at[k], half.at[k], sems.at[k]) for k in range(2)]
    for copy in copies:
        copy.start()
    slot = [jnp.minimum(block_code(owner_map, g, c) & 3, 2) for c in range(3)]
    puts = [pltpu.make_async_copy(staged.at[c], out.at[slot[c]], sems.at[2 + c]) for c in range(3)]
    copies[0].wait()
    f0[...] = half[0].reshape(1024, 128).astype(F32)
    low32 = lax.broadcasted_iota(jnp.int32, (32, 128), 1) < 64
    low8 = low32[:8]
    for q in range(2):
        for z in range(8):
            rows = f0[pl.ds(8 * q + z, 64, stride=16)].astype(jnp.bfloat16)
            buf = 8 * q + z
            d0[buf] = jnp.dot(rows.T, order[...], preferred_element_type=F32)
            for c in range(2):
                even = d0[buf, pl.ds(64 * c, 32, stride=2)]
                odd = d0[buf, pl.ds(64 * c + 1, 32, stride=2)]
                k0[c, q, pl.ds(z, 32, stride=8)] = jnp.where(low32, even, odd)
        for x2 in range(32):
            staged[1, q, :, pl.ds(128 * x2, 128)] = k0[1, q, pl.ds(8 * x2, 8)]
    puts[1].start()
    copies[1].wait()
    for x2 in range(32):
        ge, ie = (x2, 0) if x2 < 16 else ((0, 1) if x2 == 16 else (32 - x2, 1))
        go, io = (x2, 2) if x2 < 16 else (31 - x2, 3)
        even = half[1, ge, pl.ds(16 * ie, 16)].astype(F32)
        odd = half[1, go, pl.ds(16 * io, 16)].astype(F32)
        for q in range(2):
            e, o = even[8 * q : 8 * q + 8], odd[8 * q : 8 * q + 8]
            first = jnp.where(low8, e, pltpu.roll(o, 64, 1))
            third = jnp.where(low8, pltpu.roll(e, 64, 1), o)
            cols = pl.ds(128 * x2, 128)
            staged[0, q, :, cols] = first + k0[0, q, pl.ds(8 * x2, 8)]
            staged[2, q, :, cols] = third
    puts[0].start()
    puts[2].start()
    for put in puts:
        put.wait()


def body(field, levels, coefficients, failed, owner_map, velocity, diffusivity):
    smem = pl.BlockSpec(memory_space=pltpu.SMEM)
    vmem = pl.BlockSpec(memory_space=pltpu.VMEM)
    anyspace = pl.BlockSpec(memory_space=pl.ANY)
    bf = jnp.bfloat16
    dma = pltpu.SemaphoreType.DMA
    landed = pl.pallas_call(
        transform_kernel,
        out_shape=jax.ShapeDtypeStruct((2, 16, 64, 128), bf),
        in_specs=[smem] * 6 + [anyspace] * 5,
        out_specs=anyspace,
        scratch_shapes=[
            pltpu.VMEM((32, 256, 128), bf),
            pltpu.VMEM((256, 256), bf),
            pltpu.VMEM((2, 128, 1024), bf),
            pltpu.VMEM((24, 1, 1024), F32),
            pltpu.VMEM((512, 1024), bf),
            pltpu.VMEM((3, 512, 1024), bf),
            pltpu.VMEM((16, 32, 16, 128), bf),
            pltpu.VMEM((8, 32, 16, 128), bf),
            pltpu.VMEM((2, 16, 128), F32),
            pltpu.VMEM((2, 2, 7, 16, 16, 128), bf),
            pltpu.VMEM((2, 2, 7, 16, 16, 128), bf),
            pltpu.VMEM((2, 512, 128), F32),
            pltpu.VMEM((2, 2, 32, 512), bf),
            pltpu.VMEM((2, 64, 512), bf),
            pltpu.VMEM((2, 16, 2, 32, 128), bf),
            pltpu.VMEM((2, 16, 2, 32, 128), bf),
            pltpu.VMEM((64, 64, 128), bf),
            pltpu.VMEM((2, 16, 64, 128), bf),
            pltpu.VMEM((2, 2, 8, 512), F32),
            pltpu.VMEM((2, 2, 128, 128), F32),
            pltpu.SMEM((48,), jnp.int32),
            dma((6,)), dma((17,)), dma((17,)), dma((2, 2, 7)), dma((2, 2, 7)),
            dma((2, 16)), dma((2, 16)), dma((2, 16)), dma((2, 16)),
            pltpu.SemaphoreType.REGULAR,
        ],
        compiler_params=pltpu.CompilerParams(
            collective_id=0, has_side_effects=True, vmem_limit_bytes=56 * 2**20
        ),
        name="transform",
    )(
        levels, coefficients, failed, owner_map, velocity, diffusivity, field,
        jnp.asarray(mid_table()), jnp.asarray(z_bases()), jnp.asarray(z_masks()), jnp.asarray(long_table()),
    )
    return pl.pallas_call(
        place_kernel,
        out_shape=jax.ShapeDtypeStruct((3, 2, 8, 4096), F32),
        in_specs=[smem, anyspace, vmem],
        out_specs=anyspace,
        scratch_shapes=[
            pltpu.VMEM((2, 16, 64, 128), bf),
            pltpu.VMEM((1024, 128), F32),
            pltpu.VMEM((16, 128, 128), F32),
            pltpu.VMEM((2, 2, 256, 128), F32),
            pltpu.VMEM((3, 2, 8, 4096), F32),
            dma((5,)),
        ],
        compiler_params=pltpu.CompilerParams(vmem_limit_bytes=56 * 2**20),
        name="place",
    )(owner_map, landed, jnp.asarray(order_table()))


def solution(mesh):
    placed = (P("grid", "pencil", None, None), P("grid", None), P("grid"), P("grid"), P(), P(), P())
    return jax.shard_map(
        body, mesh=mesh, in_specs=placed, out_specs=P("grid", None, "pencil", None), check_vma=False
    )
```

```python
import functools
import math

import jax
import jax.numpy as jnp
import ml_dtypes
import numpy as np
from jax import lax
from jax.experimental import pallas as pl
from jax.experimental.pallas import tpu as pltpu
from jax.sharding import PartitionSpec as P

BF16 = ml_dtypes.bfloat16
F32 = jnp.float32
MESH = pl.DeviceIdType.MESH


def dft_table(length):
    positions = np.arange(length, dtype=np.int64)
    angles = (positions[:, None] * positions[None, :] % length) * (2.0 * math.pi / length)
    return np.cos(angles).astype(BF16).astype(np.float32), (-np.sin(angles)).astype(BF16).astype(np.float32)


def slot_positions(g):
    return [2 * g, 32 if g == 0 else 64 - 2 * g, 2 * g + 1, 63 - 2 * g]


@functools.cache
def mid_table():
    cos, sin = dft_table(256)
    rows = np.zeros((16, 2, 4, 2, 256), np.float32)
    for g in range(16):
        for grp in range(2):
            for i, n in enumerate(slot_positions(g)):
                rows[g, grp, i, 0] = cos[n + 64 * grp]
                rows[g, grp, i, 1] = sin[n + 64 * grp]
    rows[0, 0, 0, 1] = cos[128]
    return rows.reshape(256, 256).astype(BF16)


@functools.cache
def z_bases():
    cos, sin = dft_table(128)
    c = cos.reshape(16, 8, 128).transpose(2, 0, 1)
    s = sin.reshape(16, 8, 128).transpose(2, 0, 1)
    both = np.stack([np.stack([c, s], 2), np.stack([-s, c], 2)])
    full = np.broadcast_to(both[:, :, :, None], (2, 128, 16, 4, 2, 8))
    return full.reshape(2, 128, 1024).astype(BF16)


@functools.cache
def z_masks():
    out = np.zeros((3, 2, 2, 2, 16, 2, 2, 16), np.float32)

    def put(variant, i2, ab, sign, slot, which, scale):
        out[variant, i2, ab, which, :, sign, slot] = scale

    for variant in range(3):
        for i2 in range(2):
            if variant == 1 and i2 == 0:
                put(1, 0, 0, 0, 0, 0, 1.0)
                put(1, 0, 1, 1, 0, 0, 1.0)
                continue
            back = 1 - i2 if variant == 0 else i2
            put(variant, i2, 0, 0, i2, 0, 1.0)
            put(variant, i2, 1, 0, i2, 1, 1.0)
            put(variant, i2, 0, 1, back, 0, 1.0)
            put(variant, i2, 1, 1, back, 1, -1.0)
    return out.reshape(24, 1, 1024)


@functools.cache
def long_table():
    cos, sin = dft_table(512)
    return np.concatenate([cos, sin], axis=1).astype(BF16)


@functools.cache
def order_table():
    out = np.zeros((64, 128), np.float32)
    for g in range(16):
        for i, n in enumerate(slot_positions(g)):
            out[g * 4 + i, n] = 1.0
            out[g * 4 + i, n + 64] = 1.0
    return out.astype(BF16)


PLUS_D = (4, 3, 3, 2, 2, 1, 1)
PLUS_H = (0, 1, 0, 1, 0, 1, 0)
CLASSES = (
    tuple(8 * x + y for x in (0, 1, 6, 7) for y in (0, 1, 6, 7)),
    tuple(8 * x + y for x in (2, 3, 4, 5) for y in (0, 1, 6, 7)),
    tuple(8 * x + y for x in (0, 1, 6, 7) for y in (2, 3, 4, 5)),
)


def block_code(owner_map, owner, c):
    total = 0
    for b in CLASSES[c]:
        r = owner_map[b] - 3 * owner
        total = total + jnp.where((r >= 0) & (r < 3), 4 * b + r, 0)
    return total & 255


def transform_kernel(
    levels, coefficients, failed, owner_map, velocity, diffusivity, field, mid_tab, base_tab, mask_tab, long_tab,
    landing,
    fbuf, tbuf, ebuf, masks, tlbuf, wbuf, v, xr, xk, sb, rz, sf, lhs0, lhs1, chunk, rows, ff, sb2, flong, frow, codes,
    load_sem, xs_sem, xr_sem, zs_sem, zr_sem, ps_sem, pr_sem, gs_sem, gr_sem, row_sem,
):
    g = lax.axis_index("grid")
    p = lax.axis_index("pencil")
    zc, core = g // 2, g % 2
    py, px = p // 4, p % 4

    loads = [
        pltpu.make_async_copy(mid_tab, tbuf, load_sem.at[0]),
        pltpu.make_async_copy(field.at[0, pl.ds(0, 16)], fbuf.at[pl.ds(0, 16)], load_sem.at[1]),
        pltpu.make_async_copy(field.at[0, pl.ds(16, 16)], fbuf.at[pl.ds(16, 16)], load_sem.at[2]),
        pltpu.make_async_copy(base_tab, ebuf, load_sem.at[3]),
        pltpu.make_async_copy(mask_tab, masks, load_sem.at[4]),
        pltpu.make_async_copy(long_tab, tlbuf, load_sem.at[5]),
    ]
    for load in loads:
        load.start()

    barrier = pltpu.get_barrier_semaphore()
    for s in (2, 14, 1):
        og = 2 * lax.rem(zc + s // 2, 8) + lax.rem(core + s % 2, 2)
        pl.semaphore_signal(barrier, inc=1, device_id=(og, p), device_id_type=MESH)
    for s in (4, 8, 12, 1, 2, 3):
        op = 4 * lax.rem(py + s // 4, 4) + lax.rem(px + s % 4, 4)
        pl.semaphore_signal(barrier, inc=1, device_id=(g, op), device_id_type=MESH)

    kind = jnp.where(levels[0, 0] < levels[0, 1], 1.0, 0.0).astype(F32)
    weight = (coefficients[0] * (1 - failed[0])).astype(F32)
    loads[0].wait()

    def mid_step(k, carry):
        pair = jnp.concatenate([fbuf[2 * k], fbuf[2 * k + 1]], axis=1)
        y = jnp.dot(tbuf[...], pair, preferred_element_type=F32) * weight
        yb = y.astype(jnp.bfloat16)
        v[:, pl.ds(2 * k, 1)] = yb[:, :128].reshape(16, 1, 16, 128)
        v[:, pl.ds(2 * k + 1, 1)] = yb[:, 128:].reshape(16, 1, 16, 128)
        return carry

    loads[1].wait()
    lax.fori_loop(0, 8, mid_step, 0, unroll=4)
    loads[2].wait()
    lax.fori_loop(8, 16, mid_step, 0, unroll=4)

    xk[0] = jnp.full((16, 128), kind, F32)
    pl.semaphore_wait(barrier, 9)

    mate = (g + 1 - 2 * core, p)
    kind_copy = pltpu.make_async_remote_copy(
        xk.at[0], xk.at[1], xs_sem.at[16], xr_sem.at[16], device_id=mate, device_id_type=MESH
    )
    kind_copy.start()
    swaps = {}
    order = [(4, 0), (4, 1), (3, 1), (5, 0), (3, 0), (5, 1), (2, 1), (6, 0), (2, 0), (6, 1)]
    order += [(1, 1), (7, 0), (1, 0), (7, 1), (0, 0), (0, 1)]
    for d, h in order:
        z = lax.rem(zc + d, 8)
        swaps[d, h] = pltpu.make_async_remote_copy(
            v.at[2 * z + 1 - core, pl.ds(16 * h, 16)],
            xr.at[z, pl.ds(16 * h, 16)],
            xs_sem.at[2 * d + h],
            xr_sem.at[2 * d + h],
            device_id=mate,
            device_id_type=MESH,
        )
        if len(swaps) <= 4:
            swaps[d, h].start()
    kind_copy.wait_recv()
    other = xk[1][None]
    mine = kind
    swapped = set()

    def await_swap(d, h):
        if (d, h) not in swapped:
            swapped.add((d, h))
            swaps[d, h].wait_recv()

    def own_sum(z, at, k):
        me = v[2 * z + core, pl.ds(at, 4)].astype(F32)
        mate_part = xr[z, pl.ds(at, 4)].astype(F32)
        if k == 0:
            return me * (1.0 - mine) + mate_part * (1.0 - other)
        return me * mine + mate_part * other

    hops = {}

    def hop(k, n):
        for way in range(2):
            d = PLUS_D[n] if way == 0 else 8 - PLUS_D[n]
            h = PLUS_H[n] if way == 0 else 1 - PLUS_H[n]
            z = lax.rem(zc + d, 8)
            await_swap(d, h)
            if n >= 2:
                hops[k, way, n - 2].wait_recv()

            def add_step(a, carry):
                total = own_sum(z, 16 * h + 4 * a, k)
                if n >= 2:
                    total = total + rz[k, way, n - 2, pl.ds(4 * a, 4)].astype(F32)
                sb[k, way, n, pl.ds(4 * a, 4)] = total.astype(jnp.bfloat16)
                return carry

            lax.fori_loop(0, 4, add_step, 0)
            to = lax.rem(zc + (1 if way == 0 else 7), 8)
            hops[k, way, n] = pltpu.make_async_remote_copy(
                sb.at[k, way, n],
                rz.at[k, way, n],
                zs_sem.at[k, way, n],
                zr_sem.at[k, way, n],
                device_id=(2 * to + core, p),
                device_id_type=MESH,
            )
            hops[k, way, n].start()

    for s in range(1, 4):
        op = 4 * py + lax.rem(px + s, 4)
        pl.semaphore_signal(row_sem, inc=1, device_id=(g, op), device_id_type=MESH)

    def find_codes():
        def code_step(o, carry):
            for c in range(3):
                codes[3 * o + c] = block_code(owner_map, o, c)
            return carry

        lax.fori_loop(0, 16, code_step, 0)

    def tables():
        loads[3].wait()
        loads[4].wait()
        first = jnp.where(g == 0, 1, 0)
        for variant in range(3):
            var = variant * first
            for blk in range(4):

                def table_step(c, carry):
                    at = pl.ds(16 * c, 16)
                    me = masks[8 * var + 2 * blk]
                    mi = masks[8 * var + 2 * blk + 1]
                    val = ebuf[0, at].astype(F32) * me + ebuf[1, at].astype(F32) * mi
                    wbuf[variant, pl.ds(128 * blk + 16 * c, 16)] = val.astype(jnp.bfloat16)
                    return carry

                lax.fori_loop(0, 8, table_step, 0)

    def factors():
        lanes = lax.broadcasted_iota(jnp.int32, (8, 512), 1)
        k_long = jnp.where(lanes < 256, lanes, lanes - 512).astype(F32)
        r = lax.broadcasted_iota(jnp.int32, (128, 128), 0)
        i2, sign = (r >> 3) & 1, (r >> 4) & 1
        pair, grp = (r >> 5) & 1, (r >> 6) & 1
        pos = jnp.where(i2 == 0, 2 * g + pair, jnp.where((pair == 0) & (g == 0), 32, 64 - 2 * g - pair))
        base = jnp.where(grp == 0, -64 * sign, 64 - 192 * sign)
        k_mid = (pos + base).astype(F32)
        zi = 8 * p + (r & 7)
        k_z = jnp.where(zi < 64, zi, zi - 128).astype(F32)
        for k in range(2):
            mag = jnp.exp(diffusivity[k] * k_long * k_long * (-4.0 / 512**2))
            ph = velocity[k] * k_long * (-2.0 * math.pi / 256)
            flong[k, 0] = mag * jnp.cos(ph)
            flong[k, 1] = mag * jnp.sin(ph)
            d_mid = diffusivity[1 - k]
            v_mid = velocity[1 - k]
            mag = jnp.exp((d_mid * k_mid * k_mid + diffusivity[2] * k_z * k_z) * (-4.0 / 512**2)) * (1.0 / 4096)
            ph = (v_mid * k_mid + velocity[2] * k_z) * (-2.0 * math.pi / 256)
            frow[k, 0] = mag * jnp.cos(ph)
            frow[k, 1] = mag * jnp.sin(ph)

    def collect(k):
        for h in range(2):
            await_swap(0, h)
            a_way, b_way = (6, 5) if h == 0 else (5, 6)
            hops[k, 0, a_way].wait_recv()
            hops[k, 1, b_way].wait_recv()

            def last_step(a, carry):
                total = own_sum(zc, 16 * h + 4 * a, k)
                total = total + rz[k, 0, a_way, pl.ds(4 * a, 4)].astype(F32)
                total = total + rz[k, 1, b_way, pl.ds(4 * a, 4)].astype(F32)
                sf[k, pl.ds(256 * h + 64 * a, 64)] = total.reshape(64, 128)
                return carry

            lax.fori_loop(0, 4, last_step, 0)

    lane = lax.broadcasted_iota(jnp.int32, (64, 128), 1)
    low = lane < 64
    low32 = low[:32]
    lane32 = lane[:32] % 64
    swap = (lane32 >= 32) & (lane32 < 48) & (g == 0)

    def along_z(k):
        for grp in range(2):
            for pair in range(2):
                for e in range(4):
                    j = grp * 8 + pair * 4 + e
                    part = sf[k, pl.ds(j, 32, stride=16)].astype(jnp.bfloat16)
                    if pair == 0:
                        lhs0[k, grp, :, pl.ds(128 * e, 128)] = part
                    else:
                        lhs1[k, pl.ds(32 * grp, 32), pl.ds(128 * e, 128)] = part
        for t2 in range(4):
            cols = pl.ds(256 * t2, 256)
            wide_a = jnp.dot(lhs0[k, 0], wbuf[1, :, cols], preferred_element_type=F32)
            wide_b = jnp.dot(lhs0[k, 1], wbuf[2, :, cols], preferred_element_type=F32)
            wide_1 = jnp.dot(lhs1[k], wbuf[0, :, cols], preferred_element_type=F32)
            for t1 in range(2):
                t = 2 * t2 + t1
                part = slice(128 * t1, 128 * t1 + 128)
                ua, ub, u1 = wide_a[:, part], wide_b[:, part], wide_1[:, part]
                u1r = pltpu.roll(u1, 64, 1)
                for grp in range(2):
                    u0 = jnp.where(swap, ub, ua) if grp == 0 else jnp.where(swap, ua, ub)
                    u0r = pltpu.roll(u0, 64, 1)
                    at = slice(32 * grp, 32 * grp + 32)
                    chunk[k, 2 * t, grp] = jnp.where(low32, u0, u1r[at]).astype(jnp.bfloat16)
                    chunk[k, 2 * t + 1, grp] = jnp.where(low32, u0r, u1[at]).astype(jnp.bfloat16)

    outs = {}

    def send_lines(k):
        for s in (10, 11, 14, 9, 6, 15, 13, 7, 5, 8, 2, 12, 4, 3, 1):
            op = 4 * lax.rem(py + s // 4, 4) + lax.rem(px + s % 4, 4)
            outs[k, s] = pltpu.make_async_remote_copy(
                chunk.at[k, op],
                rows.at[k, p],
                ps_sem.at[k, s],
                pr_sem.at[k, s],
                device_id=(g, op),
                device_id_type=MESH,
            )
            outs[k, s].start()
        rows[k, pl.ds(p, 1)] = chunk[k, pl.ds(p, 1)]

    def along_long(k):
        for s in range(1, 16):
            outs[k, s].wait_recv()
        for grp in range(2):
            turned = rows[k, :, grp].reshape(512, 128).T
            for t in range(4):
                col_c = tlbuf[:, pl.ds(128 * t, 128)]
                col_s = tlbuf[:, pl.ds(512 + 128 * t, 128)]
                both = jnp.dot(turned, jnp.concatenate([col_c, col_s], axis=1), preferred_element_type=F32)
                c = both[:, :128].reshape(8, 2, 8, 128)
                sn = both[:, 128:].reshape(8, 2, 8, 128)
                re = c[:, 0] - sn[:, 1]
                im = c[:, 1] + sn[:, 0]
                rr = frow[k, 0, pl.ds(64 * grp, 64)].reshape(8, 8, 128)
                ri = frow[k, 1, pl.ds(64 * grp, 64)].reshape(8, 8, 128)
                lr = flong[k, 0, :, pl.ds(128 * t, 128)][None]
                li = flong[k, 1, :, pl.ds(128 * t, 128)][None]
                er = rr * lr - ri * li
                ei = rr * li + ri * lr
                out_re = re * er - im * ei
                out_im = re * ei + im * er
                full = jnp.stack([out_re, out_im], axis=1).reshape(2, 2, 2, 16, 128)
                spun = pltpu.roll(full.reshape(128, 128), 64, 1).reshape(2, 2, 2, 16, 128)
                for sign in range(2):
                    at = ((2 * k + grp) * 8 + t) * 2 + sign
                    ff[at] = full[:, sign].reshape(64, 128).astype(jnp.bfloat16)
                    ff[at + 8] = spun[:, sign].reshape(64, 128).astype(jnp.bfloat16)

    def piece(k, lb, gb, high):
        sign = gb >> 2
        grp = (gb & 1) ^ sign
        rot = (lb & 1) if high == 0 else 1 - (lb & 1)
        at = (((2 * k + grp) * 2 + rot) * 4 + (lb >> 1)) * 2 + sign
        return ff[at].astype(F32)

    finals = {}

    def send_pieces(k):
        for s in (8, 9, 7, 6, 10, 11, 5, 4, 12, 13, 3, 2, 14, 15, 1, 0):
            og = 2 * lax.rem(zc + s // 2, 8) + lax.rem(core + s % 2, 2)
            ca = codes[3 * og] >> 2
            cb = codes[3 * og + 1 + k] >> 2
            if k == 0:
                one, two = piece(0, ca >> 3, ca & 7, 0), piece(0, cb >> 3, cb & 7, 1)
            else:
                one, two = piece(1, ca & 7, ca >> 3, 0), piece(1, cb & 7, cb >> 3, 1)
            sb2[k, s] = jnp.where(low, one, two).astype(jnp.bfloat16)
            if s:
                copy = pltpu.make_async_remote_copy(
                    sb2.at[k, s],
                    landing.at[k, g],
                    gs_sem.at[k, s],
                    gr_sem.at[k, s],
                    device_id=(og, p),
                    device_id_type=MESH,
                )
            else:
                copy = pltpu.make_async_copy(sb2.at[k, 0], landing.at[k, g], gs_sem.at[k, 0])
            copy.start()
            finals[k, s] = copy

    hop(0, 0)
    for d, h in order[4:]:
        swaps[d, h].start()
    for k, n in ((0, 1), (1, 0)):
        hop(k, n)
    tables()
    for k, n in ((0, 2), (0, 3), (1, 1)):
        hop(k, n)
    find_codes()
    for k, n in ((0, 4), (0, 5), (1, 2)):
        hop(k, n)
    factors()
    for k, n in ((0, 6), (1, 3), (1, 4)):
        hop(k, n)
    collect(0)
    along_z(0)
    pl.semaphore_wait(row_sem, 3)
    send_lines(0)
    hop(1, 5)
    hop(1, 6)
    collect(1)
    along_z(1)
    send_lines(1)
    loads[5].wait()
    for k in range(2):
        along_long(k)
        send_pieces(k)

    for copy in finals.values():
        copy.wait()
    for copy in outs.values():
        copy.wait_send()
    for copy in hops.values():
        copy.wait_send()
    for copy in swaps.values():
        copy.wait_send()
    kind_copy.wait_send()


def place_kernel(owner_map, landed, order, out, half, f0, d0, k0, staged, sems):
    g = lax.axis_index("grid")
    copies = [pltpu.make_async_copy(landed.at[k], half.at[k], sems.at[k]) for k in range(2)]
    for copy in copies:
        copy.start()
    slot = [jnp.minimum(block_code(owner_map, g, c) & 3, 2) for c in range(3)]
    puts = [pltpu.make_async_copy(staged.at[c], out.at[slot[c]], sems.at[2 + c]) for c in range(3)]
    copies[0].wait()
    f0[...] = half[0].reshape(1024, 128).astype(F32)
    low32 = lax.broadcasted_iota(jnp.int32, (32, 128), 1) < 64
    low8 = low32[:8]
    for q in range(2):
        for z in range(8):
            rows = f0[pl.ds(8 * q + z, 64, stride=16)].astype(jnp.bfloat16)
            buf = 8 * q + z
            d0[buf] = jnp.dot(rows.T, order[...], preferred_element_type=F32)
            for c in range(2):
                even = d0[buf, pl.ds(64 * c, 32, stride=2)]
                odd = d0[buf, pl.ds(64 * c + 1, 32, stride=2)]
                k0[c, q, pl.ds(z, 32, stride=8)] = jnp.where(low32, even, odd)
        for x2 in range(32):
            staged[1, q, :, pl.ds(128 * x2, 128)] = k0[1, q, pl.ds(8 * x2, 8)]
    puts[1].start()
    copies[1].wait()
    for x2 in range(32):
        ge, ie = (x2, 0) if x2 < 16 else ((0, 1) if x2 == 16 else (32 - x2, 1))
        go, io = (x2, 2) if x2 < 16 else (31 - x2, 3)
        even = half[1, ge, pl.ds(16 * ie, 16)].astype(F32)
        odd = half[1, go, pl.ds(16 * io, 16)].astype(F32)
        for q in range(2):
            e, o = even[8 * q : 8 * q + 8], odd[8 * q : 8 * q + 8]
            first = jnp.where(low8, e, pltpu.roll(o, 64, 1))
            third = jnp.where(low8, pltpu.roll(e, 64, 1), o)
            cols = pl.ds(128 * x2, 128)
            staged[0, q, :, cols] = first + k0[0, q, pl.ds(8 * x2, 8)]
            staged[2, q, :, cols] = third
    puts[0].start()
    puts[2].start()
    for put in puts:
        put.wait()


def body(field, levels, coefficients, failed, owner_map, velocity, diffusivity):
    smem = pl.BlockSpec(memory_space=pltpu.SMEM)
    vmem = pl.BlockSpec(memory_space=pltpu.VMEM)
    anyspace = pl.BlockSpec(memory_space=pl.ANY)
    bf = jnp.bfloat16
    dma = pltpu.SemaphoreType.DMA
    landed = pl.pallas_call(
        transform_kernel,
        out_shape=jax.ShapeDtypeStruct((2, 16, 64, 128), bf),
        in_specs=[smem] * 6 + [anyspace] * 5,
        out_specs=anyspace,
        scratch_shapes=[
            pltpu.VMEM((32, 256, 128), bf),
            pltpu.VMEM((256, 256), bf),
            pltpu.VMEM((2, 128, 1024), bf),
            pltpu.VMEM((24, 1, 1024), F32),
            pltpu.VMEM((512, 1024), bf),
            pltpu.VMEM((3, 512, 1024), bf),
            pltpu.VMEM((16, 32, 16, 128), bf),
            pltpu.VMEM((8, 32, 16, 128), bf),
            pltpu.VMEM((2, 16, 128), F32),
            pltpu.VMEM((2, 2, 7, 16, 16, 128), bf),
            pltpu.VMEM((2, 2, 7, 16, 16, 128), bf),
            pltpu.VMEM((2, 512, 128), F32),
            pltpu.VMEM((2, 2, 32, 512), bf),
            pltpu.VMEM((2, 64, 512), bf),
            pltpu.VMEM((2, 16, 2, 32, 128), bf),
            pltpu.VMEM((2, 16, 2, 32, 128), bf),
            pltpu.VMEM((64, 64, 128), bf),
            pltpu.VMEM((2, 16, 64, 128), bf),
            pltpu.VMEM((2, 2, 8, 512), F32),
            pltpu.VMEM((2, 2, 128, 128), F32),
            pltpu.SMEM((48,), jnp.int32),
            dma((6,)), dma((17,)), dma((17,)), dma((2, 2, 7)), dma((2, 2, 7)),
            dma((2, 16)), dma((2, 16)), dma((2, 16)), dma((2, 16)),
            pltpu.SemaphoreType.REGULAR,
        ],
        compiler_params=pltpu.CompilerParams(
            collective_id=0, has_side_effects=True, vmem_limit_bytes=56 * 2**20
        ),
        name="transform",
    )(
        levels, coefficients, failed, owner_map, velocity, diffusivity, field,
        jnp.asarray(mid_table()), jnp.asarray(z_bases()), jnp.asarray(z_masks()), jnp.asarray(long_table()),
    )
    return pl.pallas_call(
        place_kernel,
        out_shape=jax.ShapeDtypeStruct((3, 2, 8, 4096), F32),
        in_specs=[smem, anyspace, vmem],
        out_specs=anyspace,
        scratch_shapes=[
            pltpu.VMEM((2, 16, 64, 128), bf),
            pltpu.VMEM((1024, 128), F32),
            pltpu.VMEM((16, 128, 128), F32),
            pltpu.VMEM((2, 2, 256, 128), F32),
            pltpu.VMEM((3, 2, 8, 4096), F32),
            dma((5,)),
        ],
        compiler_params=pltpu.CompilerParams(vmem_limit_bytes=56 * 2**20),
        name="place",
    )(owner_map, landed, jnp.asarray(order_table()))


def solution(mesh):
    placed = (P("grid", "pencil", None, None), P("grid", None), P("grid"), P("grid"), P(), P(), P())
    return jax.shard_map(
        body, mesh=mesh, in_specs=placed, out_specs=P("grid", None, "pencil", None), check_vma=False
    )
```
